32 devices in a mesh: dp: 4 (over y, x), seq: 8 (over z, core).
Axes of the slice: x: 2, y: 2, z: 4, core: 2. Of those that a mesh axis runs over, the one named last changes fastest.
Arguments:
- tiles: bfloat16 [4, 8192, 768], P('dp', 'seq'), may hold values from -48 to 48
- tile_count: int32 [4], P('dp'), may hold values from 4097 to 8192
- offsets: int32 [16], replicated, may hold values from 0 to 15
- w_query: bfloat16 [768, 768], replicated, may hold values from -0.375 to 0.375
- w_key: bfloat16 [768, 768], replicated, may hold values from -0.375 to 0.375
- w_value: bfloat16 [768, 768], replicated, may hold values from -0.21875 to 0.21875
- w_out: bfloat16 [768, 768], replicated, may hold values from -0.21875 to 0.21875
- cotangent: bfloat16 [4, 8192, 768], P('dp', 'seq'), may hold values from -0.046875 to 0.046875
Outputs:
- branch: bfloat16 [4, 8192, 768], P('dp', 'seq')
- grad_out: float32 [768, 768], P(None, 'seq')
The draws below stay inside these ranges and needn't reach their ends.
All inputs are finite; a program needn't handle non-finite values.
Results may differ from the reference program's by a relative error of at most 0.0095.
The reference program's roundings to bfloat16 on the way count: a program that leaves them out, or rounds other values in their place, can miss the bound.
Values may be sent and summed in bfloat16 or wider, within the bound.
A program may use at most 128 MiB of HBM per device.

```python
import jax
import jax.numpy as jnp
from jax import lax

D = 768
ATTENTION_HEADS = 16
HEAD_SIZE = 48
SEG = 1024
RATE = 16
SLIDES = 4
TOKENS = 8192


def draw_tiles(key, part):
    extent = (SLIDES, TOKENS, D)
    normal_key = jax.random.fold_in(key, 0)
    values = jax.random.truncated_normal(normal_key, -6.0, 6.0, extent, jnp.float32)
    return values.astype(jnp.bfloat16)


def plant(entries, key, least, high):
    longest = entries.shape.index(max(entries.shape))
    spots = []
    for shift in (0, 1):
        where = [jax.random.randint(jax.random.fold_in(key, axis), (), 0, length) for axis, length in enumerate(entries.shape)]
        where[longest] = (where[longest] + shift) % entries.shape[longest]
        spots.append(tuple(where))
    return entries.at[spots[0]].set(least).at[spots[1]].set(high)


def raised(drawn, key, source, target, parts, factor):
    def block_of(dim):
        return (jnp.arange(drawn.shape[dim]) // (drawn.shape[dim] // parts)).reshape((-1,) + (1,) * (drawn.ndim - 1 - dim))

    first = jax.random.permutation(key, parts)[block_of(target)]
    other_side = (block_of(target) + parts // 2) % parts
    return jnp.where((block_of(source) == first) | (block_of(source) == other_side), factor * drawn, drawn)


def block_scale(key, shape, shards, low, top_value):
    def one(dim, parts):
        draws = jax.random.uniform(jax.random.fold_in(jax.random.fold_in(key, 6), dim), (parts,), jnp.float32, low / len(shards), top_value / len(shards))
        return jnp.repeat(jnp.exp(draws), shape[dim] // parts).reshape((-1,) + (1,) * (len(shape) - dim - 1))

    factor_of = one(*shards[0])
    for cut in shards[1:]:
        factor_of = factor_of * one(*cut)
    return factor_of


def bell_draw(own_key, dims, scale, limit, pieces=(), held_as=jnp.bfloat16):
    array = jax.random.normal(own_key, dims, jnp.float32) * scale
    if len(pieces) > 0:
        array = block_scale(own_key, dims, pieces, -0.22, 0.18) * array
    return jnp.clip(array, min=-limit, max=limit).astype(held_as)


def gaussian_with(key, shape, scale, bound, pieces, heavy, kind=jnp.bfloat16):
    array = scale * jax.random.normal(key, shape, jnp.float32)
    if pieces:
        array = array * block_scale(key, shape, pieces, -0.22, 0.18)
    return jnp.clip(raised(array, jax.random.fold_in(key, 3), *heavy), -bound, bound).astype(kind)


def setup_inputs(seed: int = 0) -> dict:
    arg_keys = jax.random.split(jax.random.key(seed), 9)
    return {
        "tiles": draw_tiles(jax.random.fold_in(arg_keys[8], 71), 0),
        "tile_count": plant(jax.random.randint(arg_keys[1], (SLIDES,), TOKENS // 2 + 1, TOKENS + 1), jax.random.fold_in(arg_keys[1], 1), TOKENS // 2 + 1, TOKENS).astype(jnp.int32),
        "offsets": plant(jax.random.randint(arg_keys[2], (ATTENTION_HEADS,), 0, RATE), jax.random.fold_in(arg_keys[2], 1), 0, RATE - 1).astype(jnp.int32),
        "w_query": bell_draw(arg_keys[3], (D, D), (D // 3) ** -0.5, 0.375),
        "w_key": bell_draw(arg_keys[4], (D, D), (D // 3) ** -0.5, 0.375),
        "w_value": bell_draw(arg_keys[5], (D, D), D ** -0.5, 0.21875),
        "w_out": bell_draw(arg_keys[6], (D, D), D ** -0.5, 0.21875),
        "cotangent": gaussian_with(arg_keys[7], (SLIDES, TOKENS, D), (TOKENS * SLIDES) ** -0.5, 0.046875, ((0, 4), (1, 8)), (1, 2, 8, 2.0)),
    }


NEGATIVE_FLOOR = -1e30


def project(inputs, weight):
    return jnp.dot(inputs, weight, preferred_element_type=jnp.float32).astype(jnp.bfloat16)


def select_rows(tensor, offsets):
    segment_height = tensor.shape[0]
    grouped = tensor.reshape(segment_height // RATE, RATE, ATTENTION_HEADS, HEAD_SIZE).astype(jnp.float32)
    onehot = (jnp.arange(RATE, dtype=jnp.int32)[:, None] == offsets[None, :]).astype(jnp.float32)
    return jnp.einsum('arhd,rh->ahd', grouped, onehot).astype(jnp.bfloat16)


def segment_attention(blocks):
    query_seg, key_seg, value_seg, alive_seg = blocks
    scores = jnp.einsum('qhd,khd->hqk', query_seg.astype(jnp.float32), key_seg.astype(jnp.float32)) * (HEAD_SIZE ** -0.5)
    scores = jnp.where(alive_seg[None, None, :], scores, NEGATIVE_FLOOR)
    maxima = jnp.max(scores, axis=-1)
    weights = jnp.exp(scores - maxima[..., None])
    totals = jnp.sum(weights, axis=-1)
    rounded = lax.optimization_barrier(weights.astype(jnp.bfloat16))
    weighted = jnp.einsum('hqk,khd->qhd', rounded.astype(jnp.float32), value_seg.astype(jnp.float32))
    return maxima.T, totals.T, weighted


def combine(local, dilated_branch, offsets, is_live):
    local_max, local_total, local_sum = local
    dilated_row_max, dilated_value_total, dilated_row_sum = dilated_branch
    segment_height = local_max.shape[0]
    dilation_match = jnp.arange(RATE, dtype=jnp.int32)[:, None] == offsets[None, :]
    dense_row_max = jnp.where(dilation_match[None], dilated_row_max[:, None, :], NEGATIVE_FLOOR).reshape(segment_height, ATTENTION_HEADS)
    dense_value_total = jnp.where(dilation_match[None], dilated_value_total[:, None, :], 0.0).reshape(segment_height, ATTENTION_HEADS)
    dense_row_sum = jnp.where(dilation_match[None, :, :, None], dilated_row_sum[:, None], 0.0).reshape(segment_height, ATTENTION_HEADS, HEAD_SIZE)
    top = jnp.maximum(local_max, dense_row_max)
    near = jnp.exp(local_max - top)
    far = jnp.exp(dense_row_max - top)
    attn = (near[..., None] * local_sum + far[..., None] * dense_row_sum) / (near * local_total + far * dense_value_total)[..., None]
    attn = jnp.where(is_live[:, None, None], attn, 0.0)
    return attn.reshape(segment_height, D).astype(jnp.bfloat16)


def reference(tiles, tile_count, offsets, w_query, w_key, w_value, w_out, cotangent):
    outputs = []
    gradient = jnp.zeros((D, D), jnp.float32)
    segments = TOKENS // SEG
    picked = TOKENS // RATE
    for slide in range(SLIDES):
        inputs = tiles[slide]
        live_count = tile_count[slide]
        query_proj = project(inputs, w_query).reshape(TOKENS, ATTENTION_HEADS, HEAD_SIZE)
        key_proj = project(inputs, w_key).reshape(TOKENS, ATTENTION_HEADS, HEAD_SIZE)
        value_proj = project(inputs, w_value).reshape(TOKENS, ATTENTION_HEADS, HEAD_SIZE)
        is_live = jnp.arange(TOKENS, dtype=jnp.int32) < live_count
        local = lax.map(segment_attention, (query_proj.reshape(segments, SEG, ATTENTION_HEADS, HEAD_SIZE), key_proj.reshape(segments, SEG, ATTENTION_HEADS, HEAD_SIZE), value_proj.reshape(segments, SEG, ATTENTION_HEADS, HEAD_SIZE), is_live.reshape(segments, SEG)))
        local = (local[0].reshape(TOKENS, ATTENTION_HEADS), local[1].reshape(TOKENS, ATTENTION_HEADS), local[2].reshape(TOKENS, ATTENTION_HEADS, HEAD_SIZE))
        query_sel = select_rows(query_proj, offsets).transpose(1, 0, 2)
        key_sel = select_rows(key_proj, offsets).transpose(1, 0, 2)
        value_sel = select_rows(value_proj, offsets).transpose(1, 0, 2)

        def head_attention(blocks):
            query_head, key_head, value_head, offset = blocks
            key_live = jnp.arange(picked, dtype=jnp.int32) * RATE + offset < live_count
            scores = jnp.dot(query_head, key_head.T, preferred_element_type=jnp.float32) * (HEAD_SIZE ** -0.5)
            scores = jnp.where(key_live[None, :], scores, NEGATIVE_FLOOR)
            maxima = jnp.max(scores, axis=-1)
            weights = jnp.exp(scores - maxima[:, None])
            totals = jnp.sum(weights, axis=-1)
            weighted = jnp.dot(weights.astype(jnp.bfloat16), value_head, preferred_element_type=jnp.float32)
            return maxima, totals, weighted

        dilated_branch = lax.map(head_attention, (query_sel, key_sel, value_sel, offsets))
        dilated_branch = (dilated_branch[0].T, dilated_branch[1].T, dilated_branch[2].transpose(1, 0, 2))
        attn = combine(local, dilated_branch, offsets, is_live)
        outputs.append(jnp.dot(attn, w_out, preferred_element_type=jnp.float32).astype(jnp.bfloat16))
        gradient = gradient + jnp.dot(attn.T, cotangent[slide], preferred_element_type=jnp.float32)
    return jnp.stack(outputs), gradient
```

```python
import functools

import jax
import jax.numpy as jnp
from jax import lax
from jax.experimental import pallas as pl
from jax.experimental.pallas import tpu as pltpu
from jax.sharding import PartitionSpec as P

ATTENTION_HEADS = 16
HEAD_SIZE = 48
SEG = 1024
RATE = 16
NEGATIVE_FLOOR = -1e30
LOG2_SCALE = 1.4426950408889634 / HEAD_SIZE**0.5
PAD = 16
SPAN = 2 * HEAD_SIZE
PARTS = 4
LANES = 128
MESH = pl.DeviceIdType.MESH
BF16 = jnp.bfloat16
F32 = jnp.float32
VMEM = pl.BlockSpec(memory_space=pltpu.VMEM)
SMEM = pl.BlockSpec(memory_space=pltpu.SMEM)


def dot(a, b, ca=1, cb=0):
    return lax.dot_general(a, b, (((ca,), (cb,)), ((), ())), preferred_element_type=F32)


def head_rows(head):
    return pl.ds(pl.multiple_of(head * HEAD_SIZE, PAD), HEAD_SIZE)


def scaled_query(query):
    scaled = query.astype(F32) * LOG2_SCALE
    high = scaled.astype(BF16)
    low = (scaled - high.astype(F32)).astype(BF16)
    return jnp.concatenate([high, low, jnp.ones((PAD, query.shape[1]), BF16)], 0)


def masked_key(key, dead):
    row = lax.broadcasted_iota(jnp.int32, (PAD, key.shape[1]), 0)
    mask = jnp.where(dead & (row == 0), NEGATIVE_FLOOR, 0.0).astype(BF16)
    return jnp.concatenate([key, key, mask], 0)


def counted_value(value):
    return jnp.concatenate([value, jnp.ones((PAD, value.shape[1]), BF16)], 0)


def lanes(width):
    return lax.broadcasted_iota(jnp.int32, (PAD, width), 1)


def pair_rows(pair):
    return pl.ds(pl.multiple_of(pair * SPAN, PAD), SPAN)


def grid(shape, axis):
    return lax.broadcasted_iota(jnp.int32, shape, axis)


def pair_offset(lane, picked, offsets, pair):
    first = lane < picked
    return jnp.where(first, lane, lane - picked) * RATE + jnp.where(first, offsets[2 * pair], offsets[2 * pair + 1])


def pick_pair(pair, core, offsets, q, k, v, chosen, queries, onehots):
    length = q.shape[1]
    block = chosen.shape[1]
    picked = block // 2
    rows = pair_rows(pair)
    target = pair_offset(grid((1, block), 1), picked, offsets, pair)
    onehot = jnp.where(grid((length, block), 0) == target, 1.0, 0.0).astype(BF16)
    onehots[pair] = onehot
    part = dot(jnp.concatenate([q[rows, :], k[rows, :], v[rows, :]], 0), onehot)
    left = grid((SPAN, block), 1) < picked
    top = grid((SPAN, block), 0) < HEAD_SIZE
    queries[pair, :SPAN, :] = jnp.where(left == top, part[:SPAN], 0.0).astype(BF16)
    side = jnp.where(grid((PAD, block), 1) < picked, 0, 1)
    queries[pair, SPAN:, :] = jnp.where(grid((PAD, block), 0) == side, 1.0, 0.0).astype(BF16)
    keys, values = part[SPAN : 2 * SPAN], part[2 * SPAN :]
    front = jnp.where(core == 0, keys, values)
    back = jnp.where(core == 0, values, keys)
    front = jnp.where(top, front, pltpu.roll(front, picked, 1))
    back = jnp.where(top, pltpu.roll(back, picked, 1), back)
    chosen[rows, :] = jnp.where(left, front, back).astype(BF16)


def dilated_pair(pair, me, live, offsets, k, v, near, attn, gathered, queries, onehots):
    length = k.shape[1]
    spots, block = gathered.shape[1], gathered.shape[3]
    picked = block // 2
    far = spots * block
    rows = pair_rows(pair)
    left = grid((SPAN, block), 1) < picked
    keys, values = [k[rows, :]], [v[rows, :]]
    for n in range(spots):
        even, odd = gathered[0, n, rows, :], gathered[1, n, rows, :]
        keys.append(jnp.where(left, even, odd))
        values.append(jnp.where(left, odd, even))
    row = grid((PAD, length), 0)
    own = grid((PAD, length), 1) + me * length
    near_mask = jnp.where((own >= live) & (row < 2), NEGATIVE_FLOOR, 0.0).astype(BF16)
    row = grid((PAD, far), 0)
    spot = RATE * grid((PAD, far), 1) + jnp.where(row == 0, offsets[2 * pair], offsets[2 * pair + 1])
    far_mask = jnp.where((spot >= live) & (row < 2), NEGATIVE_FLOOR, 0.0).astype(BF16)
    mask = jnp.concatenate([near_mask, far_mask], 1)
    key = jnp.concatenate([jnp.concatenate(keys, 1), mask], 0)
    value = counted_value(jnp.concatenate(values, 1))
    scores = dot(key, queries[pair], 0, 0)
    peak = jnp.max(scores, axis=0, keepdims=True)
    weights = jnp.exp2((scores - peak) * LOG2_SCALE).astype(BF16)
    parts = [weights[:length]]
    for n in range(spots):
        start = length + n * block
        parts += [weights[start + picked : start + block], weights[start : start + picked]]
    total = dot(value, jnp.concatenate(parts, 0))
    token = pair_offset(grid((1, block), 1), picked, offsets, pair) + me * length
    factor = jnp.where(token < live, 1.0, 0.0) / total[SPAN : SPAN + 1]
    top = grid((SPAN, block), 0) < HEAD_SIZE
    part = jnp.where(left == top, total[:SPAN] * factor, 0.0).astype(BF16)
    spread = dot(part, onehots[pair], 1, 1)
    attn[rows, :] = (near[rows, :].astype(F32) + spread).astype(BF16)


def prepare(head, dead, q, k, keys, scaled):
    rows = head_rows(head)
    scaled[...] = scaled_query(q[rows, :])
    keys[...] = masked_key(k[rows, :], dead).T


def local_stage(score, weigh, total_of, dead, offsets, v, near, keys, scaled, peaks, scores, weights):
    length = keys.shape[0]
    half = length // 2
    step = length // PARTS
    run, total = None, None
    if weigh is not None:
        peak = peaks[weigh]
    if total_of is not None:
        head, index = total_of
        rows = head_rows(head)
        value = counted_value(v[rows, :])
    for part in range(PARTS):
        cut = slice(part * step, (part + 1) * step)
        if score is not None:
            here = dot(keys[cut, :], scaled[:, score * half : (score + 1) * half])
            scores[score][cut, :] = here
            top = jnp.max(here.reshape(step // 8, 8, half), axis=0)
            run = top if run is None else jnp.maximum(run, top)
        if weigh is not None:
            shifted = scores[weigh][cut, :].reshape(step // 8, 8, half) - peak[None]
            weights[weigh][cut, :] = jnp.exp2(shifted.reshape(step, half)).astype(BF16)
        if total_of is not None:
            piece = dot(value[:, cut], weights[index][cut, :])
            total = piece if total is None else total + piece
    if total_of is not None:
        lane = grid((1, half), 1) + index * half
        drop = dead[:1, index * half : (index + 1) * half] | (lane % RATE == offsets[head])
        factor = jnp.where(drop, 0.0, 1.0) / total[HEAD_SIZE : HEAD_SIZE + 1]
        near[rows, index * half : (index + 1) * half] = (total[:HEAD_SIZE] * factor).astype(BF16)
    if score is not None:
        peaks[score] = jnp.broadcast_to(jnp.max(run, axis=0, keepdims=True), (8, half))


def attention_kernel(
    shards, slides, fused, live, offsets, x, wq, wk, wv, w_out, cot, branch, grad, q, k, v, near, attn, chosen,
    gathered, queries, onehots, keys, scaled, peaks, s0, s1, w0, w1, gather_send, gather_recv, *scratch
):
    width, length = q.shape
    picked = length // RATE
    block = 2 * picked
    half = ATTENTION_HEADS // 2
    lead = half - 1
    me = lax.axis_index("seq")
    slide = lax.axis_index("dp")
    spots = shards // 2
    spot, core = me // 2, me % 2
    ahead = [lax.rem(spot + n, spots) for n in range(spots)]
    others = [lax.rem(slide + n, slides) for n in range(slides)]
    partner = {"seq": me + 1 - 2 * core}
    line = [{"seq": 2 * ahead[n] + core} for n in range(spots)]
    peers = [partner] + line[1:]
    if fused:
        peers = peers + [{"dp": others[n]} for n in range(1, slides)]
    barrier = pltpu.get_barrier_semaphore()
    for peer in peers:
        pl.semaphore_signal(barrier, inc=1, device_id=peer, device_id_type=MESH)

    def copy(src, dst, send, recv, peer):
        item = pltpu.make_async_remote_copy(
            src_ref=src, dst_ref=dst, send_sem=send, recv_sem=recv, device_id=peer, device_id_type=MESH
        )
        item.start()
        return item

    tiles = x[...]
    for weight, out in ((wk, k), (wv, v), (wq, q)):
        out[...] = dot(weight[...].T, tiles, 1, 1).astype(BF16)

    def pick(pair, carry):
        pick_pair(pair, core, offsets, q, k, v, chosen, queries, onehots)
        return carry

    lax.fori_loop(0, half, pick, 0, unroll=2)
    pl.semaphore_wait(barrier, len(peers))

    def relay(src, origin, way):
        slot = gathered.at[core, origin]
        return pltpu.make_async_remote_copy(
            src_ref=src,
            dst_ref=slot,
            send_sem=gather_send.at[way, origin],
            recv_sem=gather_recv.at[1 if way == 2 else 0, origin],
            device_id=({"seq": me + 2}, {"seq": me - 2}, partner)[way],
            device_id_type=MESH,
        )

    def arrival(origin):
        slot = gathered.at[1 - core, origin]
        return pltpu.make_async_remote_copy(
            src_ref=slot,
            dst_ref=slot,
            send_sem=gather_send.at[2, origin],
            recv_sem=gather_recv.at[1, origin],
            device_id=partner,
            device_id_type=MESH,
        )

    @pl.when(spot < spots - 1)
    def _():
        relay(chosen, spot, 0).start()

    @pl.when(spot > 0)
    def _():
        relay(chosen, spot, 1).start()

    relay(chosen, spot, 2).start()
    gathered[core, spot] = chosen[...]

    def pass_on(step):
        @pl.when(spot >= step)
        def _():
            origin = spot - step
            slot = gathered.at[core, origin]
            relay(slot, origin, 0).wait_recv()

            @pl.when(spot < spots - 1)
            def _():
                relay(slot, origin, 0).start()

            relay(slot, origin, 2).start()

        @pl.when(spot + step < spots)
        def _():
            origin = spot + step
            slot = gathered.at[core, origin]
            relay(slot, origin, 1).wait_recv()

            @pl.when(spot > 0)
            def _():
                relay(slot, origin, 1).start()

            relay(slot, origin, 2).start()

    def end_gather():
        for origin in range(spots):
            slot = gathered.at[core, origin]

            @pl.when((spot >= origin) & (spot < spots - 1))
            def _():
                relay(slot, origin, 0).wait_send()

            @pl.when((spot <= origin) & (spot > 0))
            def _():
                relay(slot, origin, 1).wait_send()

            relay(slot, origin, 2).wait_send()

    dead = lanes(length) + me * length >= live[0]
    scores, weights = (s0, s1), (w0, w1)

    def advance(score, weigh, total_of):
        local_stage(score, weigh, total_of, dead, offsets, v, near, keys, scaled, peaks, scores, weights)

    w1[...] = jnp.ones(w1.shape, BF16)
    prepare(0, dead, q, k, keys, scaled)
    advance(0, None, None)

    def local(head, carry):
        @pl.when(head > -1)
        def _():
            advance(1, 0, (jnp.maximum(head - 1, 0), 1))

        @pl.when(head > -2)
        def _():
            prepare(jnp.minimum(head + 1, ATTENTION_HEADS - 1), dead, q, k, keys, scaled)
            advance(0, 1, (head, 0))

        return carry

    def dilated(start, stop):
        def step(index, carry):
            for n in range(2):
                dilated_pair(
                    start + 2 * index + n, me, live[0], offsets, k, v, near, attn, gathered, queries, onehots
                )
            return carry

        lax.fori_loop(0, (stop - start) // 2, step, 0)

    cuts = [n * (lead - 1) // (spots - 1) for n in range(spots)]
    for step in range(1, spots):
        lax.fori_loop(cuts[step - 1], cuts[step], local, 0)
        pass_on(step)
    lax.fori_loop(cuts[-1], half + 1, local, 0)
    for origin in range(spots):
        arrival(origin).wait_recv()
    dilated(0, half // 2)

    def gradient(rows):
        return dot(attn[rows, :], cot[...]).astype(BF16).T

    if not fused:
        lax.fori_loop(half + 1, ATTENTION_HEADS, local, 0)
        advance(None, None, (ATTENTION_HEADS - 1, 1))
        dilated(half // 2, half)
        grad[...] = gradient(slice(0, width))
        branch[...] = dot(attn[...].T, w_out[...]).astype(BF16)
        end_gather()
        return

    stage, pair_in, chip, slide_in, chip_sum, line_in, final = scratch[:7]
    pair_send, pair_recv, slide_send, slide_recv, line_send, line_recv, last_send, last_recv = scratch[7:]
    columns = width // shards
    wide = width // 2
    count = wide // LANES
    part = columns * count // slides
    turns = list(range(1, spots)) + [0]
    pair, across, along, last = {}, {}, {}, {}

    def open_pair(g):
        share = gradient(slice(g * wide, (g + 1) * wide))
        for shard in range(shards):
            for tile in range(count):
                stage[g, shard % 2, shard // 2, tile * columns : (tile + 1) * columns, :] = share[
                    shard * columns : (shard + 1) * columns, tile * LANES : (tile + 1) * LANES
                ]
        for n in turns:
            pair[g, n] = copy(
                stage.at[g, 1 - core, ahead[n]],
                pair_in.at[g, n],
                pair_send.at[g, n],
                pair_recv.at[g, n],
                partner,
            )

    def open_across(g):
        for n in turns:
            pair[g, n].wait_recv()
            mine = stage[g, core, ahead[n]].astype(F32) + pair_in[g, n].astype(F32)
            for p in range(slides):
                chip[g, n, p] = mine[p * part : (p + 1) * part].astype(BF16)
            for j in range(1, slides):
                across[g, n, j] = copy(
                    chip.at[g, n, others[j]],
                    slide_in.at[g, n, j - 1],
                    slide_send.at[g, n, j - 1],
                    slide_recv.at[g, n, j - 1],
                    {"dp": others[j]},
                )

    def open_along(g):
        for n in turns:
            total = chip[g, n, slide].astype(F32)
            for j in range(1, slides):
                across[g, n, j].wait_recv()
                total = total + slide_in[g, n, j - 1].astype(F32)
            chip_sum[g, n] = total.astype(BF16)
            if n:
                along[g, n] = copy(
                    chip_sum.at[g, n],
                    line_in.at[g, n - 1],
                    line_send.at[g, n - 1],
                    line_recv.at[g, n - 1],
                    line[n],
                )

    def open_last(g):
        total = chip_sum[g, 0].astype(F32)
        for n in range(1, spots):
            along[g, n].wait_recv()
            total = total + line_in[g, n - 1].astype(F32)
        final[g, slide] = total.astype(BF16)
        for j in range(1, slides):
            last[g, j] = copy(
                final.at[g, slide],
                final.at[g, slide],
                last_send.at[g, j - 1],
                last_recv.at[g, j - 1],
                {"dp": others[j]},
            )

    def close(g):
        for j in range(1, slides):
            last[g, j].wait_recv()
        full = jnp.concatenate([final[g, p].astype(F32) for p in range(slides)], 0)
        for tile in range(count):
            rows = slice(g * wide + tile * LANES, g * wide + (tile + 1) * LANES)
            grad[rows, :] = full[tile * columns : (tile + 1) * columns].T

    open_pair(0)
    lax.fori_loop(half + 1, half + 4, local, 0)
    open_across(0)
    lax.fori_loop(half + 4, ATTENTION_HEADS, local, 0)
    open_along(0)
    advance(None, None, (ATTENTION_HEADS - 1, 1))
    dilated(half // 2, half)
    open_last(0)
    open_pair(1)
    open_across(1)
    branch[...] = dot(attn[...].T, w_out[...]).astype(BF16)
    open_along(1)
    close(0)
    open_last(1)
    close(1)
    end_gather()
    for group in (pair.values(), across.values(), along.values(), last.values()):
        for item in group:
            item.wait_send()


def body(shards, slides, tiles, tile_count, offsets, w_query, w_key, w_value, w_out, cotangent):
    inputs = tiles[0]
    length, width = inputs.shape
    assert length == SEG and shards % 2 == 0
    spots = shards // 2
    columns = width // shards
    rows = columns * (width // 2 // LANES)
    fused = columns % PAD == 0 and rows % (8 * slides) == 0 and spots > 1 and slides > 1
    dma = pltpu.SemaphoreType.DMA
    held = pltpu.VMEM((width, length), BF16)
    block = 2 * (length // RATE)
    scratch = [held] * 5 + [
        pltpu.VMEM((width, block), BF16),
        pltpu.VMEM((2, spots, width, block), BF16),
        pltpu.VMEM((ATTENTION_HEADS // 2, SPAN + PAD, block), BF16),
        pltpu.VMEM((ATTENTION_HEADS // 2, length, block), BF16),
        pltpu.VMEM((length, SPAN + PAD), BF16),
        pltpu.VMEM((SPAN + PAD, length), BF16),
        pltpu.VMEM((2, 8, length // 2), F32),
        pltpu.VMEM((length, length // 2), F32),
        pltpu.VMEM((length, length // 2), F32),
        pltpu.VMEM((length, length // 2), BF16),
        pltpu.VMEM((length, length // 2), BF16),
        dma((3, spots)),
        dma((2, spots)),
    ]
    grad_type = jax.ShapeDtypeStruct((width, width), BF16)
    if fused:
        part = rows // slides
        grad_type = jax.ShapeDtypeStruct((width, columns), F32)
        scratch += [
            pltpu.VMEM((2, 2, spots, rows, LANES), BF16),
            pltpu.VMEM((2, spots, rows, LANES), BF16),
            pltpu.VMEM((2, spots, slides, part, LANES), BF16),
            pltpu.VMEM((2, spots, slides - 1, part, LANES), BF16),
            pltpu.VMEM((2, spots, part, LANES), BF16),
            pltpu.VMEM((2, spots - 1, part, LANES), BF16),
            pltpu.VMEM((2, slides, part, LANES), BF16),
        ]
        for shape in ((2, spots), (2, spots, slides - 1), (2, spots - 1), (2, slides - 1)):
            scratch += [dma(shape), dma(shape)]
    branch, grad = pl.pallas_call(
        functools.partial(attention_kernel, shards, slides, fused),
        out_shape=(jax.ShapeDtypeStruct((length, width), BF16), grad_type),
        in_specs=[SMEM] * 2 + [VMEM] * 6,
        out_specs=(VMEM,) * 2,
        scratch_shapes=scratch,
        compiler_params=pltpu.CompilerParams(
            vmem_limit_bytes=60 << 20, collective_id=0, has_side_effects=True
        ),
    )(tile_count, offsets, inputs, w_query, w_key, w_value, w_out, cotangent[0])
    if not fused:
        share = lax.psum_scatter(grad, "seq", scatter_dimension=0, tiled=True)
        grad = lax.psum(share, "dp").astype(F32).T
    return (branch[None], grad)


def solution(mesh):
    in_specs = (P("dp", "seq", None), P("dp"), P(), P(), P(), P(), P(), P("dp", "seq", None))
    out_specs = (P("dp", "seq", None), P(None, "seq"))
    run = functools.partial(body, mesh.shape["seq"], mesh.shape["dp"])
    return jax.shard_map(run, mesh=mesh, in_specs=in_specs, out_specs=out_specs, check_vma=False)
```

```python
import functools

import jax
import jax.numpy as jnp
from jax import lax
from jax.experimental import pallas as pl
from jax.experimental.pallas import tpu as pltpu
from jax.sharding import PartitionSpec as P

ATTENTION_HEADS = 16
HEAD_SIZE = 48
SEG = 1024
RATE = 16
NEGATIVE_FLOOR = -1e30
LOG2_SCALE = 1.4426950408889634 / HEAD_SIZE**0.5
PAD = 16
SPAN = 2 * HEAD_SIZE
PARTS = 4
LANES = 128
MESH = pl.DeviceIdType.MESH
BF16 = jnp.bfloat16
F32 = jnp.float32
VMEM = pl.BlockSpec(memory_space=pltpu.VMEM)
SMEM = pl.BlockSpec(memory_space=pltpu.SMEM)


def dot(a, b, ca=1, cb=0):
    return lax.dot_general(a, b, (((ca,), (cb,)), ((), ())), preferred_element_type=F32)


def head_rows(head):
    return pl.ds(pl.multiple_of(head * HEAD_SIZE, PAD), HEAD_SIZE)


def scaled_query(query):
    scaled = query.astype(F32) * LOG2_SCALE
    high = scaled.astype(BF16)
    low = (scaled - high.astype(F32)).astype(BF16)
    return jnp.concatenate([high, low, jnp.ones((PAD, query.shape[1]), BF16)], 0)


def masked_key(key, dead):
    row = lax.broadcasted_iota(jnp.int32, (PAD, key.shape[1]), 0)
    mask = jnp.where(dead & (row == 0), NEGATIVE_FLOOR, 0.0).astype(BF16)
    return jnp.concatenate([key, key, mask], 0)


def counted_value(value):
    return jnp.concatenate([value, jnp.ones((PAD, value.shape[1]), BF16)], 0)


def lanes(width):
    return lax.broadcasted_iota(jnp.int32, (PAD, width), 1)


def pair_rows(pair):
    return pl.ds(pl.multiple_of(pair * SPAN, PAD), SPAN)


def grid(shape, axis):
    return lax.broadcasted_iota(jnp.int32, shape, axis)


def pair_offset(lane, picked, offsets, pair):
    first = lane < picked
    return jnp.where(first, lane, lane - picked) * RATE + jnp.where(first, offsets[2 * pair], offsets[2 * pair + 1])


def pick_pair(pair, core, offsets, q, k, v, chosen, queries, onehots):
    length = q.shape[1]
    block = chosen.shape[1]
    picked = block // 2
    rows = pair_rows(pair)
    target = pair_offset(grid((1, block), 1), picked, offsets, pair)
    onehot = jnp.where(grid((length, block), 0) == target, 1.0, 0.0).astype(BF16)
    onehots[pair] = onehot
    part = dot(jnp.concatenate([q[rows, :], k[rows, :], v[rows, :]], 0), onehot)
    left = grid((SPAN, block), 1) < picked
    top = grid((SPAN, block), 0) < HEAD_SIZE
    queries[pair, :SPAN, :] = jnp.where(left == top, part[:SPAN], 0.0).astype(BF16)
    side = jnp.where(grid((PAD, block), 1) < picked, 0, 1)
    queries[pair, SPAN:, :] = jnp.where(grid((PAD, block), 0) == side, 1.0, 0.0).astype(BF16)
    keys, values = part[SPAN : 2 * SPAN], part[2 * SPAN :]
    front = jnp.where(core == 0, keys, values)
    back = jnp.where(core == 0, values, keys)
    front = jnp.where(top, front, pltpu.roll(front, picked, 1))
    back = jnp.where(top, pltpu.roll(back, picked, 1), back)
    chosen[rows, :] = jnp.where(left, front, back).astype(BF16)


def dilated_pair(pair, me, live, offsets, k, v, near, attn, gathered, queries, onehots):
    length = k.shape[1]
    spots, block = gathered.shape[1], gathered.shape[3]
    picked = block // 2
    far = spots * block
    rows = pair_rows(pair)
    left = grid((SPAN, block), 1) < picked
    keys, values = [k[rows, :]], [v[rows, :]]
    for n in range(spots):
        even, odd = gathered[0, n, rows, :], gathered[1, n, rows, :]
        keys.append(jnp.where(left, even, odd))
        values.append(jnp.where(left, odd, even))
    row = grid((PAD, length), 0)
    own = grid((PAD, length), 1) + me * length
    near_mask = jnp.where((own >= live) & (row < 2), NEGATIVE_FLOOR, 0.0).astype(BF16)
    row = grid((PAD, far), 0)
    spot = RATE * grid((PAD, far), 1) + jnp.where(row == 0, offsets[2 * pair], offsets[2 * pair + 1])
    far_mask = jnp.where((spot >= live) & (row < 2), NEGATIVE_FLOOR, 0.0).astype(BF16)
    mask = jnp.concatenate([near_mask, far_mask], 1)
    key = jnp.concatenate([jnp.concatenate(keys, 1), mask], 0)
    value = counted_value(jnp.concatenate(values, 1))
    scores = dot(key, queries[pair], 0, 0)
    peak = jnp.max(scores, axis=0, keepdims=True)
    weights = jnp.exp2((scores - peak) * LOG2_SCALE).astype(BF16)
    parts = [weights[:length]]
    for n in range(spots):
        start = length + n * block
        parts += [weights[start + picked : start + block], weights[start : start + picked]]
    total = dot(value, jnp.concatenate(parts, 0))
    token = pair_offset(grid((1, block), 1), picked, offsets, pair) + me * length
    factor = jnp.where(token < live, 1.0, 0.0) / total[SPAN : SPAN + 1]
    top = grid((SPAN, block), 0) < HEAD_SIZE
    part = jnp.where(left == top, total[:SPAN] * factor, 0.0).astype(BF16)
    spread = dot(part, onehots[pair], 1, 1)
    attn[rows, :] = (near[rows, :].astype(F32) + spread).astype(BF16)


def prepare(head, dead, q, k, keys, scaled):
    rows = head_rows(head)
    scaled[...] = scaled_query(q[rows, :])
    keys[...] = masked_key(k[rows, :], dead).T


def local_stage(score, weigh, total_of, dead, offsets, v, near, keys, scaled, peaks, scores, weights):
    length = keys.shape[0]
    half = length // 2
    step = length // PARTS
    run, total = None, None
    if weigh is not None:
        peak = peaks[weigh]
    if total_of is not None:
        head, index = total_of
        rows = head_rows(head)
        value = counted_value(v[rows, :])
    for part in range(PARTS):
        cut = slice(part * step, (part + 1) * step)
        if score is not None:
            here = dot(keys[cut, :], scaled[:, score * half : (score + 1) * half])
            scores[score][cut, :] = here
            top = jnp.max(here.reshape(step // 8, 8, half), axis=0)
            run = top if run is None else jnp.maximum(run, top)
        if weigh is not None:
            shifted = scores[weigh][cut, :].reshape(step // 8, 8, half) - peak[None]
            weights[weigh][cut, :] = jnp.exp2(shifted.reshape(step, half)).astype(BF16)
        if total_of is not None:
            piece = dot(value[:, cut], weights[index][cut, :])
            total = piece if total is None else total + piece
    if total_of is not None:
        lane = grid((1, half), 1) + index * half
        drop = dead[:1, index * half : (index + 1) * half] | (lane % RATE == offsets[head])
        factor = jnp.where(drop, 0.0, 1.0) / total[HEAD_SIZE : HEAD_SIZE + 1]
        near[rows, index * half : (index + 1) * half] = (total[:HEAD_SIZE] * factor).astype(BF16)
    if score is not None:
        peaks[score] = jnp.broadcast_to(jnp.max(run, axis=0, keepdims=True), (8, half))


def attention_kernel(
    shards, slides, groups, live, offsets, x_hbm, wq_hbm, wk_hbm, wv_hbm, wo_hbm, cot_hbm, branch_hbm, grad,
    x, wq, wk, wv, w_out, cot, branch, loads, q, k, v, near, attn, chosen, gathered, queries, onehots,
    keys, scaled, peaks, s0, s1, w0, w1, line_out, line_here, pair_out, pair_here, *scratch
):
    width, length = q.shape
    pairs = ATTENTION_HEADS // 2
    half = pairs // 2
    cut = half * SPAN
    me = lax.axis_index("seq")
    slide = lax.axis_index("dp")
    spots = shards // 2
    spot, core = me // 2, me % 2
    ahead = [lax.rem(spot + n, spots) for n in range(spots)]
    behind = [lax.rem(spot + spots - n, spots) for n in range(spots)]
    others = [lax.rem(slide + n, slides) for n in range(slides)]
    partner = {"seq": me + 1 - 2 * core}
    line = [{"seq": 2 * ahead[n] + core} for n in range(spots)]
    peers = [partner] + line[1:]
    if groups:
        peers = peers + [{"dp": others[n]} for n in range(1, slides)]
    barrier = pltpu.get_barrier_semaphore()
    for peer in peers:
        pl.semaphore_signal(barrier, inc=1, device_id=peer, device_id_type=MESH)

    def load(index):
        source, target = ((x_hbm, x), (wk_hbm, wk), (wv_hbm, wv), (wq_hbm, wq), (cot_hbm, cot), (wo_hbm, w_out))[index]
        return pltpu.make_async_copy(source, target, loads.at[index])

    for index in range(4):
        load(index).start()

    def copy(src, dst, send, recv, peer):
        item = pltpu.make_async_remote_copy(
            src_ref=src, dst_ref=dst, send_sem=send, recv_sem=recv, device_id=peer, device_id_type=MESH
        )
        item.start()
        return item

    load(0).wait()
    for index, (weight, out) in enumerate(((wk, k), (wv, v), (wq, q))):
        load(index + 1).wait()
        out[...] = dot(weight[...].T, x[...], 1, 1).astype(BF16)
    for index in (4, 5):
        load(index).start()

    def pick(pair, carry):
        pick_pair(pair, core, offsets, q, k, v, chosen, queries, onehots)
        return carry

    def slab(g):
        return pl.ds(g * cut, cut)

    def sent(g, n):
        return pltpu.make_async_remote_copy(
            src_ref=chosen.at[slab(g)],
            dst_ref=gathered.at[core, spot, slab(g)],
            send_sem=line_out.at[g, n - 1],
            recv_sem=line_here.at[g, n - 1],
            device_id=line[n],
            device_id_type=MESH,
        )

    def shared(g, n, side):
        slot = gathered.at[side, behind[n], slab(g)]
        return pltpu.make_async_remote_copy(
            src_ref=slot if n else chosen.at[slab(g)],
            dst_ref=slot,
            send_sem=pair_out.at[g, n],
            recv_sem=pair_here.at[g, n],
            device_id=partner,
            device_id_type=MESH,
        )

    def send_own(g):
        for n in range(1, spots):
            sent(g, n).start()
        shared(g, 0, core).start()

    def share(g):
        for n in range(1, spots):
            slot = gathered.at[core, behind[n], slab(g)]
            pltpu.make_async_remote_copy(
                src_ref=slot,
                dst_ref=slot,
                send_sem=line_out.at[g, n - 1],
                recv_sem=line_here.at[g, n - 1],
                device_id=line[n],
                device_id_type=MESH,
            ).wait_recv()
            shared(g, n, core).start()

    def arrived(g):
        for n in range(spots):
            shared(g, n, 1 - core).wait_recv()

    def end_gather():
        for g in range(2):
            for n in range(spots):
                shared(g, n, core).wait_send()
                if n:
                    sent(g, n).wait_send()

    lax.fori_loop(0, half, pick, 0, unroll=2)
    pl.semaphore_wait(barrier, len(peers))
    send_own(0)
    lax.fori_loop(half, pairs, pick, 0, unroll=2)
    gathered[core, spot] = chosen[...]

    dead = lanes(length) + me * length >= live[0]
    scores, weights = (s0, s1), (w0, w1)

    def advance(score, weigh, total_of):
        local_stage(score, weigh, total_of, dead, offsets, v, near, keys, scaled, peaks, scores, weights)

    def local(head, carry):
        @pl.when(head > -1)
        def _():
            advance(1, 0, (jnp.maximum(head - 1, 0), 1))

        @pl.when(head > -2)
        def _():
            prepare(jnp.minimum(head + 1, ATTENTION_HEADS - 1), dead, q, k, keys, scaled)
            advance(0, 1, (head, 0))

        return carry

    def dilated(pair):
        dilated_pair(pair, me, live[0], offsets, k, v, near, attn, gathered, queries, onehots)

    def dilated_half(start):
        def step(index, carry):
            dilated(start + 2 * index)
            dilated(start + 2 * index + 1)
            return carry

        lax.fori_loop(0, half // 2, step, 0)

    def gradient(rows):
        return dot(attn[rows, :], cot[...]).astype(BF16).T

    stages = []
    used = 0
    for first, last in groups:
        count = 11 if stages else 15
        stages.append(scratch[used : used + count])
        used += count
    columns = width // shards

    def open_pair(g):
        first, last = groups[g]
        stage, pair_in, send, recv = stages[g][:4]
        whole = gradient(slice(first * LANES, last * LANES))
        for shard in range(shards):
            for tile in range(last - first):
                stage[shard % 2, shard // 2, tile * columns : (tile + 1) * columns, :] = whole[
                    shard * columns : (shard + 1) * columns, tile * LANES : (tile + 1) * LANES
                ]
        moves[g, 0] = [copy(stage.at[1 - core], pair_in, send.at[0], recv.at[0], partner)]

    def open_across(g):
        stage, pair_in = stages[g][:2]
        chip, slide_in, send, recv = stages[g][4:6] + stages[g][9:11]
        part = chip.shape[2]
        moves[g, 0][0].wait_recv()
        for n in range(spots):
            mine = stage[core, n].astype(F32) + pair_in[n].astype(F32)
            for p in range(slides):
                chip[p, n] = mine[p * part : (p + 1) * part].astype(BF16)
        moves[g, 1] = [
            copy(chip.at[others[j]], slide_in.at[j - 1], send.at[j - 1], recv.at[j - 1], {"dp": others[j]})
            for j in range(1, slides)
        ]

    def open_along(g):
        chip, slide_in, chip_sum, line_in, send, recv = stages[g][4:8] + stages[g][11:13]
        for item in moves[g, 1]:
            item.wait_recv()
        for n in range(spots):
            total = chip[slide, n].astype(F32)
            for j in range(1, slides):
                total = total + slide_in[j - 1, n].astype(F32)
            chip_sum[n] = total.astype(BF16)
        moves[g, 2] = [
            copy(chip_sum.at[ahead[n]], line_in.at[n - 1], send.at[n - 1], recv.at[n - 1], line[n])
            for n in range(1, spots)
        ]

    def open_last(g):
        chip_sum, line_in, final, send, recv = stages[g][6:9] + stages[g][13:15]
        total = chip_sum[spot].astype(F32)
        for n in range(1, spots):
            moves[g, 2][n - 1].wait_recv()
            total = total + line_in[n - 1].astype(F32)
        final[slide] = total.astype(BF16)
        moves[g, 3] = [
            copy(final.at[slide], final.at[slide], send.at[j - 1], recv.at[j - 1], {"dp": others[j]})
            for j in range(1, slides)
        ]

    def close(g):
        first, last = groups[g]
        final = stages[g][8]
        for item in moves[g, 3]:
            item.wait_recv()
        full = jnp.concatenate([final[p].astype(F32) for p in range(slides)], 0)
        for tile in range(last - first):
            at = (first + tile) * LANES
            grad[:, at : at + LANES] = full[tile * columns : (tile + 1) * columns]

    def short_along(g):
        stage, pair_in = stages[g][:2]
        chip_sum, line_in = stages[g][4:6]
        send, recv = stages[g][7:9]
        moves[g, 0][0].wait_recv()
        for n in range(spots):
            chip_sum[n] = (stage[core, n].astype(F32) + pair_in[n].astype(F32)).astype(BF16)
        moves[g, 2] = [
            copy(chip_sum.at[ahead[n]], line_in.at[n - 1], send.at[n - 1], recv.at[n - 1], line[n])
            for n in range(1, spots)
        ]

    def short_last(g):
        chip_sum, line_in, final = stages[g][4:7]
        send, recv = stages[g][9:11]
        total = chip_sum[spot].astype(F32)
        for n in range(1, spots):
            moves[g, 2][n - 1].wait_recv()
            total = total + line_in[n - 1].astype(F32)
        final[slide] = total.astype(BF16)
        moves[g, 3] = [
            copy(final.at[slide], final.at[slide], send.at[j - 1], recv.at[j - 1], {"dp": others[j]})
            for j in range(1, slides)
        ]

    def short_close(g):
        first, last = groups[g]
        final = stages[g][6]
        for item in moves[g, 3]:
            item.wait_recv()
        full = final[0].astype(F32)
        for p in range(1, slides):
            full = full + final[p].astype(F32)
        for tile in range(last - first):
            at = (first + tile) * LANES
            grad[:, at : at + LANES] = full[tile * columns : (tile + 1) * columns]

    moves = {}
    store = pltpu.make_async_copy(branch, branch_hbm, loads.at[6])

    def project(part, parts):
        rows = slice(part * length // parts, (part + 1) * length // parts)
        branch[rows, :] = dot(attn[:, rows].T, w_out[...]).astype(BF16)

    w1[...] = jnp.ones(w1.shape, BF16)
    prepare(0, dead, q, k, keys, scaled)
    advance(0, None, None)
    todo = {n: [] for n in range(ATTENTION_HEADS + 1)}
    ready = ATTENTION_HEADS // 2 + 2
    late = ATTENTION_HEADS - 1
    todo[ATTENTION_HEADS // 4].append(functools.partial(send_own, 1))
    todo[ready - 1].append(functools.partial(share, 0))
    todo[ready] += [functools.partial(arrived, 0), functools.partial(dilated_half, 0)]
    todo[late - 1].append(functools.partial(share, 1))
    todo[late].append(functools.partial(arrived, 1))
    if groups:
        todo[ready] += [load(4).wait, functools.partial(open_pair, 0)]
        todo[ready + 1].append(functools.partial(open_across, 0))
    done = 0
    for at in range(ATTENTION_HEADS + 1):
        if todo[at]:
            lax.fori_loop(done, at, local, 0)
            done = at
            for action in todo[at]:
                action()

    def rest(pair, carry):
        dilated(pair)
        return carry

    if not groups:
        lax.fori_loop(done, ATTENTION_HEADS, local, 0)
        advance(None, None, (ATTENTION_HEADS - 1, 1))
        dilated_half(half)
        load(4).wait()
        load(5).wait()
        grad[...] = gradient(slice(0, width))
        project(0, 1)
        store.start()
        end_gather()
        store.wait()
        return

    lax.fori_loop(half, pairs - 1, rest, 0, unroll=3)
    open_pair(1)
    open_along(0)
    lax.fori_loop(done, ATTENTION_HEADS, local, 0)
    short_along(1)
    advance(None, None, (ATTENTION_HEADS - 1, 1))
    dilated(pairs - 1)
    open_pair(2)
    load(5).wait()
    project(0, 2)
    short_along(2)
    open_last(0)
    project(1, 2)
    store.start()
    short_last(1)
    short_last(2)
    close(0)
    short_close(1)
    end_gather()
    short_close(2)
    for items in moves.values():
        for item in items:
            item.wait_send()
    store.wait()


def move_kernel(branch, grad, branch_out, grad_out, held, small, come, leave):
    length = branch.shape[0]
    parts = come.shape[0] - 1
    pieces = [(grad, small, grad_out)]
    for n in range(parts):
        rows = pl.ds(n * (length // parts), length // parts)
        pieces.append((branch.at[rows], held.at[rows], branch_out.at[rows]))
    loads = [pltpu.make_async_copy(a, b, come.at[n]) for n, (a, b, c) in enumerate(pieces)]
    stores = [pltpu.make_async_copy(b, c, leave.at[n]) for n, (a, b, c) in enumerate(pieces)]
    for item in loads:
        item.start()
    for item, out in zip(loads, stores):
        item.wait()
        out.start()
    for item in stores:
        item.wait()


def body(shards, slides, tiles, tile_count, offsets, w_query, w_key, w_value, w_out, cotangent):
    inputs = tiles[0]
    length, width = inputs.shape
    assert length == SEG and shards % 2 == 0
    spots = shards // 2
    columns = width // shards
    fused = columns % PAD == 0 and columns % (8 * slides) == 0 and spots > 1 and slides > 1
    pairs = ATTENTION_HEADS // 2
    ends = [0] + [count * SPAN // LANES for count in (pairs // 2, pairs - 1, pairs)]
    groups = list(zip(ends[:-1], ends[1:])) if fused else []
    dma = pltpu.SemaphoreType.DMA
    held = pltpu.VMEM((width, length), BF16)
    square = pltpu.VMEM((width, width), BF16)
    tall = pltpu.VMEM((length, width), BF16)
    block = 2 * (length // RATE)
    chunk = length // 2
    scratch = [tall] + [square] * 4 + [tall] * 2 + [dma((7,))] + [held] * 5 + [
        pltpu.VMEM((width, block), BF16),
        pltpu.VMEM((2, spots, width, block), BF16),
        pltpu.VMEM((pairs, SPAN + PAD, block), BF16),
        pltpu.VMEM((pairs, length, block), BF16),
        pltpu.VMEM((length, SPAN + PAD), BF16),
        pltpu.VMEM((SPAN + PAD, length), BF16),
        pltpu.VMEM((2, 8, chunk), F32),
        pltpu.VMEM((length, chunk), F32),
        pltpu.VMEM((length, chunk), F32),
        pltpu.VMEM((length, chunk), BF16),
        pltpu.VMEM((length, chunk), BF16),
        dma((2, spots - 1)),
        dma((2, spots - 1)),
        dma((2, spots)),
        dma((2, spots)),
    ]
    grad_type = jax.ShapeDtypeStruct((width, width), BF16)
    if fused:
        grad_type = jax.ShapeDtypeStruct((columns, width), F32)
    for first, last in groups:
        rows = columns * (last - first)
        part = rows // slides
        scratch += [
            pltpu.VMEM((2, spots, rows, LANES), BF16),
            pltpu.VMEM((spots, rows, LANES), BF16),
            dma((1,)),
            dma((1,)),
        ]
        if first == 0:
            scratch += [
                pltpu.VMEM((slides, spots, part, LANES), BF16),
                pltpu.VMEM((slides - 1, spots, part, LANES), BF16),
                pltpu.VMEM((spots, part, LANES), BF16),
                pltpu.VMEM((spots - 1, part, LANES), BF16),
                pltpu.VMEM((slides, part, LANES), BF16),
            ]
            counts = (slides - 1, spots - 1, slides - 1)
        else:
            scratch += [
                pltpu.VMEM((spots, rows, LANES), BF16),
                pltpu.VMEM((spots - 1, rows, LANES), BF16),
                pltpu.VMEM((slides, rows, LANES), BF16),
            ]
            counts = (spots - 1, slides - 1)
        for count in counts:
            scratch += [dma((count,)), dma((count,))]
    hbm = pl.BlockSpec(memory_space=pl.ANY)
    branch_type = jax.ShapeDtypeStruct((length, width), BF16)
    branch, grad = pl.pallas_call(
        functools.partial(attention_kernel, shards, slides, groups),
        out_shape=(branch_type, grad_type),
        in_specs=[SMEM] * 2 + [hbm] * 6,
        out_specs=(hbm, VMEM),
        scratch_shapes=scratch,
        compiler_params=pltpu.CompilerParams(
            vmem_limit_bytes=60 << 20, collective_id=0, has_side_effects=True
        ),
    )(tile_count, offsets, inputs, w_query, w_key, w_value, w_out, cotangent[0])
    if fused:
        branch, grad = pl.pallas_call(
            move_kernel,
            out_shape=(branch_type, grad_type),
            in_specs=[hbm] * 2,
            out_specs=(hbm, hbm),
            scratch_shapes=[tall, pltpu.VMEM((columns, width), F32), dma((9,)), dma((9,))],
        )(branch, grad)
        grad = grad.T
    else:
        share = lax.psum_scatter(grad, "seq", scatter_dimension=0, tiled=True)
        grad = lax.psum(share, "dp").astype(F32).T
    return (branch[None], grad)


def solution(mesh):
    in_specs = (P("dp", "seq", None), P("dp"), P(), P(), P(), P(), P(), P("dp", "seq", None))
    out_specs = (P("dp", "seq", None), P(None, "seq"))
    run = functools.partial(body, mesh.shape["seq"], mesh.shape["dp"])
    return jax.shard_map(run, mesh=mesh, in_specs=in_specs, out_specs=out_specs, check_vma=False)
```

```python
import functools

import jax
import jax.numpy as jnp
from jax import lax
from jax.experimental import pallas as pl
from jax.experimental.pallas import tpu as pltpu
from jax.sharding import PartitionSpec as P

ATTENTION_HEADS = 16
HEAD_SIZE = 48
SEG = 1024
RATE = 16
NEGATIVE_FLOOR = -1e30
LOG2_SCALE = 1.4426950408889634 / HEAD_SIZE**0.5
PAD = 16
SPAN = 2 * HEAD_SIZE
PARTS = 8
LANES = 128
MESH = pl.DeviceIdType.MESH
BF16 = jnp.bfloat16
F32 = jnp.float32
VMEM = pl.BlockSpec(memory_space=pltpu.VMEM)
SMEM = pl.BlockSpec(memory_space=pltpu.SMEM)


def dot(a, b, ca=1, cb=0):
    return lax.dot_general(a, b, (((ca,), (cb,)), ((), ())), preferred_element_type=F32)


def head_rows(head):
    return pl.ds(pl.multiple_of(head * HEAD_SIZE, PAD), HEAD_SIZE)


def scaled_query(query):
    scaled = query.astype(F32) * LOG2_SCALE
    high = scaled.astype(BF16)
    low = (scaled - high.astype(F32)).astype(BF16)
    return jnp.concatenate([high, low, jnp.ones((PAD, query.shape[1]), BF16)], 0)


def masked_key(key, dead):
    row = lax.broadcasted_iota(jnp.int32, (PAD, key.shape[1]), 0)
    mask = jnp.where(dead & (row == 0), NEGATIVE_FLOOR, 0.0).astype(BF16)
    return jnp.concatenate([key, key, mask], 0)


def counted_value(value):
    return jnp.concatenate([value, jnp.ones((PAD, value.shape[1]), BF16)], 0)


def lanes(width):
    return lax.broadcasted_iota(jnp.int32, (PAD, width), 1)


def pair_rows(pair):
    return pl.ds(pl.multiple_of(pair * SPAN, PAD), SPAN)


def grid(shape, axis):
    return lax.broadcasted_iota(jnp.int32, shape, axis)


def pair_offset(lane, picked, offsets, pair):
    first = lane < picked
    return jnp.where(first, lane, lane - picked) * RATE + jnp.where(first, offsets[2 * pair], offsets[2 * pair + 1])


def pick_pair(pair, core, offsets, q, k, v, chosen, queries, onehots):
    length = q.shape[1]
    block = chosen.shape[1]
    picked = block // 2
    rows = pair_rows(pair)
    target = pair_offset(grid((1, block), 1), picked, offsets, pair)
    onehot = jnp.where(grid((length, block), 0) == target, 1.0, 0.0).astype(BF16)
    onehots[pair] = onehot
    part = dot(jnp.concatenate([q[rows, :], k[rows, :], v[rows, :]], 0), onehot)
    left = grid((SPAN, block), 1) < picked
    top = grid((SPAN, block), 0) < HEAD_SIZE
    queries[pair, :SPAN, :] = jnp.where(left == top, part[:SPAN], 0.0).astype(BF16)
    side = jnp.where(grid((PAD, block), 1) < picked, 0, 1)
    queries[pair, SPAN:, :] = jnp.where(grid((PAD, block), 0) == side, 1.0, 0.0).astype(BF16)
    keys, values = part[SPAN : 2 * SPAN], part[2 * SPAN :]
    front = jnp.where(core == 0, keys, values)
    back = jnp.where(core == 0, values, keys)
    front = jnp.where(top, front, pltpu.roll(front, picked, 1))
    back = jnp.where(top, pltpu.roll(back, picked, 1), back)
    chosen[rows, :] = jnp.where(left, front, back).astype(BF16)


def dilated_pair(pair, me, live, offsets, k, v, near, attn, gathered, queries, onehots):
    length = k.shape[1]
    spots, block = gathered.shape[1], gathered.shape[3]
    picked = block // 2
    far = spots * block
    rows = pair_rows(pair)
    left = grid((SPAN, block), 1) < picked
    keys, values = [k[rows, :]], [v[rows, :]]
    for n in range(spots):
        even, odd = gathered[0, n, rows, :], gathered[1, n, rows, :]
        keys.append(jnp.where(left, even, odd))
        values.append(jnp.where(left, odd, even))
    row = grid((PAD, length), 0)
    own = grid((PAD, length), 1) + me * length
    near_mask = jnp.where((own >= live) & (row < 2), NEGATIVE_FLOOR, 0.0).astype(BF16)
    row = grid((PAD, far), 0)
    spot = RATE * grid((PAD, far), 1) + jnp.where(row == 0, offsets[2 * pair], offsets[2 * pair + 1])
    far_mask = jnp.where((spot >= live) & (row < 2), NEGATIVE_FLOOR, 0.0).astype(BF16)
    mask = jnp.concatenate([near_mask, far_mask], 1)
    key = jnp.concatenate([jnp.concatenate(keys, 1), mask], 0)
    value = counted_value(jnp.concatenate(values, 1))
    scores = dot(key, queries[pair], 0, 0)
    peak = jnp.max(scores, axis=0, keepdims=True)
    weights = jnp.exp2((scores - peak) * LOG2_SCALE).astype(BF16)
    parts = [weights[:length]]
    for n in range(spots):
        start = length + n * block
        parts += [weights[start + picked : start + block], weights[start : start + picked]]
    total = dot(value, jnp.concatenate(parts, 0))
    token = pair_offset(grid((1, block), 1), picked, offsets, pair) + me * length
    factor = jnp.where(token < live, 1.0, 0.0) / total[SPAN : SPAN + 1]
    top = grid((SPAN, block), 0) < HEAD_SIZE
    part = jnp.where(left == top, total[:SPAN] * factor, 0.0).astype(BF16)
    spread = dot(part, onehots[pair], 1, 1)
    attn[rows, :] = (near[rows, :].astype(F32) + spread).astype(BF16)


def prepare(head, slot, dead, q, k, keys, scaled):
    rows = head_rows(head)
    scaled[slot] = scaled_query(q[rows, :])
    keys[slot] = masked_key(k[rows, :], dead).T


def local_stage(score, weigh, total_of, dead, offsets, v, near, keys, scaled, peaks, scores, weights):
    length = near.shape[1]
    step = length // PARTS
    run, total = None, None
    if weigh is not None:
        peak = peaks[weigh]
    if total_of is not None:
        head, slot = total_of
        rows = head_rows(head)
        value = counted_value(v[rows, :])
    for part in range(PARTS):
        cut = slice(part * step, (part + 1) * step)
        if score is not None:
            here = dot(keys[score, cut, :], scaled[score])
            scores[score][cut, :] = here
            top = jnp.max(here.reshape(step // 8, 8, length), axis=0)
            run = top if run is None else jnp.maximum(run, top)
        if weigh is not None:
            shifted = scores[weigh][cut, :].reshape(step // 8, 8, length) - peak[None]
            weights[weigh][cut, :] = jnp.exp2(shifted.reshape(step, length)).astype(BF16)
        if total_of is not None:
            piece = dot(value[:, cut], weights[slot][cut, :])
            total = piece if total is None else total + piece
    if total_of is not None:
        drop = dead[:1] | (grid((1, length), 1) % RATE == offsets[head])
        factor = jnp.where(drop, 0.0, 1.0) / total[HEAD_SIZE : HEAD_SIZE + 1]
        near[rows, :] = (total[:HEAD_SIZE] * factor).astype(BF16)
    if score is not None:
        peaks[score] = jnp.broadcast_to(jnp.max(run, axis=0, keepdims=True), (8, length))


def attention_kernel(
    shards, slides, groups, live, offsets, x_hbm, wq_hbm, wk_hbm, wv_hbm, wo_hbm, cot_hbm, branch_hbm, grad,
    x, wq, wk, wv, w_out, cot, branch, loads, q, k, v, near, attn, chosen, gathered, queries, onehots,
    keys, scaled, peaks, s0, s1, w0, w1, line_out, line_here, pair_out, pair_here, *scratch
):
    width, length = q.shape
    pairs = ATTENTION_HEADS // 2
    half = pairs // 2
    cut = half * SPAN
    me = lax.axis_index("seq")
    slide = lax.axis_index("dp")
    spots = shards // 2
    spot, core = me // 2, me % 2
    ahead = [lax.rem(spot + n, spots) for n in range(spots)]
    behind = [lax.rem(spot + spots - n, spots) for n in range(spots)]
    others = [lax.rem(slide + n, slides) for n in range(slides)]
    partner = {"seq": me + 1 - 2 * core}
    line = [{"seq": 2 * ahead[n] + core} for n in range(spots)]
    peers = [partner] + line[1:]
    if groups:
        peers = peers + [{"dp": others[n]} for n in range(1, slides)]
    barrier = pltpu.get_barrier_semaphore()
    for peer in peers:
        pl.semaphore_signal(barrier, inc=1, device_id=peer, device_id_type=MESH)

    def load(index):
        source, target = ((x_hbm, x), (wk_hbm, wk), (wv_hbm, wv), (wq_hbm, wq), (cot_hbm, cot), (wo_hbm, w_out))[index]
        return pltpu.make_async_copy(source, target, loads.at[index])

    for index in range(4):
        load(index).start()

    def copy(src, dst, send, recv, peer):
        item = pltpu.make_async_remote_copy(
            src_ref=src, dst_ref=dst, send_sem=send, recv_sem=recv, device_id=peer, device_id_type=MESH
        )
        item.start()
        return item

    load(0).wait()
    for index, (weight, out) in enumerate(((wk, k), (wv, v), (wq, q))):
        load(index + 1).wait()
        out[...] = dot(weight[...].T, x[...], 1, 1).astype(BF16)
    for index in (4, 5):
        load(index).start()

    def pick(pair, carry):
        pick_pair(pair, core, offsets, q, k, v, chosen, queries, onehots)
        return carry

    def slab(g):
        return pl.ds(g * cut, cut)

    def sent(g, n):
        return pltpu.make_async_remote_copy(
            src_ref=chosen.at[slab(g)],
            dst_ref=gathered.at[core, spot, slab(g)],
            send_sem=line_out.at[g, n - 1],
            recv_sem=line_here.at[g, n - 1],
            device_id=line[n],
            device_id_type=MESH,
        )

    def shared(g, n, side):
        slot = gathered.at[side, behind[n], slab(g)]
        return pltpu.make_async_remote_copy(
            src_ref=slot if n else chosen.at[slab(g)],
            dst_ref=slot,
            send_sem=pair_out.at[g, n],
            recv_sem=pair_here.at[g, n],
            device_id=partner,
            device_id_type=MESH,
        )

    def send_own(g):
        for n in range(1, spots):
            sent(g, n).start()
        shared(g, 0, core).start()

    def share(g):
        for n in range(1, spots):
            slot = gathered.at[core, behind[n], slab(g)]
            pltpu.make_async_remote_copy(
                src_ref=slot,
                dst_ref=slot,
                send_sem=line_out.at[g, n - 1],
                recv_sem=line_here.at[g, n - 1],
                device_id=line[n],
                device_id_type=MESH,
            ).wait_recv()
            shared(g, n, core).start()

    def arrived(g):
        for n in range(spots):
            shared(g, n, 1 - core).wait_recv()

    def end_gather():
        for g in range(2):
            for n in range(spots):
                shared(g, n, core).wait_send()
                if n:
                    sent(g, n).wait_send()

    lax.fori_loop(0, half, pick, 0, unroll=2)
    pl.semaphore_wait(barrier, len(peers))
    send_own(0)
    lax.fori_loop(half, pairs, pick, 0, unroll=2)
    gathered[core, spot] = chosen[...]

    dead = lanes(length) + me * length >= live[0]
    scores, weights = (s0, s1), (w0, w1)

    def advance(score, weigh, total_of):
        local_stage(score, weigh, total_of, dead, offsets, v, near, keys, scaled, peaks, scores, weights)

    def block(head, slot):
        prepare(jnp.minimum(head + 2, ATTENTION_HEADS - 2 + slot), slot, dead, q, k, keys, scaled)
        advance(1 - slot, slot, (jnp.maximum(head - 1, 0), 1 - slot))

    def both(index, carry):
        @pl.when(index > -1)
        def _():
            block(2 * index, 0)

        @pl.when(index > -2)
        def _():
            block(2 * index + 1, 1)

        return carry

    def local(start, stop):
        if start % 2 and start < stop:
            block(start, 1)
            start += 1
        lax.fori_loop(start // 2, stop // 2, both, 0)
        if stop % 2 and start < stop:
            block(stop - 1, 0)

    def dilated(pair):
        dilated_pair(pair, me, live[0], offsets, k, v, near, attn, gathered, queries, onehots)

    def dilated_half(start):
        def step(index, carry):
            dilated(start + 2 * index)
            dilated(start + 2 * index + 1)
            return carry

        lax.fori_loop(0, half // 2, step, 0)

    def gradient(rows):
        return dot(attn[rows, :], cot[...]).astype(BF16).T

    stages = []
    used = 0
    for first, last in groups:
        count = 11 if stages else 15
        stages.append(scratch[used : used + count])
        used += count
    columns = width // shards

    def open_pair(g):
        first, last = groups[g]
        stage, pair_in, send, recv = stages[g][:4]
        whole = gradient(slice(first * LANES, last * LANES))
        for shard in range(shards):
            for tile in range(last - first):
                stage[shard % 2, shard // 2, tile * columns : (tile + 1) * columns, :] = whole[
                    shard * columns : (shard + 1) * columns, tile * LANES : (tile + 1) * LANES
                ]
        moves[g, 0] = [copy(stage.at[1 - core], pair_in, send.at[0], recv.at[0], partner)]

    def open_across(g):
        stage, pair_in = stages[g][:2]
        chip, slide_in, send, recv = stages[g][4:6] + stages[g][9:11]
        part = chip.shape[2]
        moves[g, 0][0].wait_recv()
        for n in range(spots):
            mine = stage[core, n].astype(F32) + pair_in[n].astype(F32)
            for p in range(slides):
                chip[p, n] = mine[p * part : (p + 1) * part].astype(BF16)
        moves[g, 1] = [
            copy(chip.at[others[j]], slide_in.at[j - 1], send.at[j - 1], recv.at[j - 1], {"dp": others[j]})
            for j in range(1, slides)
        ]

    def open_along(g):
        chip, slide_in, chip_sum, line_in, send, recv = stages[g][4:8] + stages[g][11:13]
        for item in moves[g, 1]:
            item.wait_recv()
        for n in range(spots):
            total = chip[slide, n].astype(F32)
            for j in range(1, slides):
                total = total + slide_in[j - 1, n].astype(F32)
            chip_sum[n] = total.astype(BF16)
        moves[g, 2] = [
            copy(chip_sum.at[ahead[n]], line_in.at[n - 1], send.at[n - 1], recv.at[n - 1], line[n])
            for n in range(1, spots)
        ]

    def open_last(g):
        chip_sum, line_in, final, send, recv = stages[g][6:9] + stages[g][13:15]
        total = chip_sum[spot].astype(F32)
        for n in range(1, spots):
            moves[g, 2][n - 1].wait_recv()
            total = total + line_in[n - 1].astype(F32)
        final[slide] = total.astype(BF16)
        moves[g, 3] = [
            copy(final.at[slide], final.at[slide], send.at[j - 1], recv.at[j - 1], {"dp": others[j]})
            for j in range(1, slides)
        ]

    def close(g):
        first, last = groups[g]
        final = stages[g][8]
        for item in moves[g, 3]:
            item.wait_recv()
        full = jnp.concatenate([final[p].astype(F32) for p in range(slides)], 0)
        for tile in range(last - first):
            at = (first + tile) * LANES
            grad[:, at : at + LANES] = full[tile * columns : (tile + 1) * columns]

    def short_along(g):
        stage, pair_in = stages[g][:2]
        chip_sum, line_in = stages[g][4:6]
        send, recv = stages[g][7:9]
        moves[g, 0][0].wait_recv()
        for n in range(spots):
            chip_sum[n] = (stage[core, n].astype(F32) + pair_in[n].astype(F32)).astype(BF16)
        moves[g, 2] = [
            copy(chip_sum.at[ahead[n]], line_in.at[n - 1], send.at[n - 1], recv.at[n - 1], line[n])
            for n in range(1, spots)
        ]

    def short_last(g):
        chip_sum, line_in, final = stages[g][4:7]
        send, recv = stages[g][9:11]
        total = chip_sum[spot].astype(F32)
        for n in range(1, spots):
            moves[g, 2][n - 1].wait_recv()
            total = total + line_in[n - 1].astype(F32)
        final[slide] = total.astype(BF16)
        moves[g, 3] = [
            copy(final.at[slide], final.at[slide], send.at[j - 1], recv.at[j - 1], {"dp": others[j]})
            for j in range(1, slides)
        ]

    def short_close(g):
        first, last = groups[g]
        final = stages[g][6]
        for item in moves[g, 3]:
            item.wait_recv()
        full = final[0].astype(F32)
        for p in range(1, slides):
            full = full + final[p].astype(F32)
        for tile in range(last - first):
            at = (first + tile) * LANES
            grad[:, at : at + LANES] = full[tile * columns : (tile + 1) * columns]

    moves = {}
    store = pltpu.make_async_copy(branch, branch_hbm, loads.at[6])

    def project(part, parts):
        rows = slice(part * length // parts, (part + 1) * length // parts)
        branch[rows, :] = dot(attn[:, rows].T, w_out[...]).astype(BF16)

    w1[...] = jnp.ones(w1.shape, BF16)
    prepare(0, 0, dead, q, k, keys, scaled)
    prepare(1, 1, dead, q, k, keys, scaled)
    advance(0, None, None)
    todo = {n: [] for n in range(ATTENTION_HEADS + 1)}
    ready = ATTENTION_HEADS // 2 + 3
    late = ATTENTION_HEADS - 1
    todo[ATTENTION_HEADS // 4].append(functools.partial(send_own, 1))
    todo[ready - 1].append(functools.partial(share, 0))
    todo[ready] += [functools.partial(arrived, 0), functools.partial(dilated_half, 0)]
    todo[late - 1].append(functools.partial(share, 1))
    todo[late].append(functools.partial(arrived, 1))
    if groups:
        todo[ready] += [load(4).wait, functools.partial(open_pair, 0)]
        todo[ready + 1].append(functools.partial(open_across, 0))
    done = 0
    for at in range(ATTENTION_HEADS + 1):
        if todo[at]:
            local(done, at)
            done = at
            for action in todo[at]:
                action()

    def rest(pair, carry):
        dilated(pair)
        return carry

    if not groups:
        local(done, ATTENTION_HEADS)
        advance(None, None, (ATTENTION_HEADS - 1, 1))
        dilated_half(half)
        load(4).wait()
        load(5).wait()
        grad[...] = gradient(slice(0, width))
        project(0, 1)
        store.start()
        end_gather()
        store.wait()
        return

    lax.fori_loop(half, pairs - 1, rest, 0, unroll=3)
    open_pair(1)
    open_along(0)
    local(done, ATTENTION_HEADS)
    short_along(1)
    advance(None, None, (ATTENTION_HEADS - 1, 1))
    dilated(pairs - 1)
    open_pair(2)
    load(5).wait()
    project(0, 2)
    short_along(2)
    open_last(0)
    project(1, 2)
    store.start()
    short_last(1)
    short_last(2)
    close(0)
    short_close(1)
    end_gather()
    short_close(2)
    for items in moves.values():
        for item in items:
            item.wait_send()
    store.wait()


def move_kernel(branch, grad, branch_out, grad_out, held, small, come, leave):
    length = branch.shape[0]
    parts = come.shape[0] - 1
    pieces = [(grad, small, grad_out)]
    for n in range(parts):
        rows = pl.ds(n * (length // parts), length // parts)
        pieces.append((branch.at[rows], held.at[rows], branch_out.at[rows]))
    loads = [pltpu.make_async_copy(a, b, come.at[n]) for n, (a, b, c) in enumerate(pieces)]
    stores = [pltpu.make_async_copy(b, c, leave.at[n]) for n, (a, b, c) in enumerate(pieces)]
    for item in loads:
        item.start()
    for item, out in zip(loads, stores):
        item.wait()
        out.start()
    for item in stores:
        item.wait()


def body(shards, slides, tiles, tile_count, offsets, w_query, w_key, w_value, w_out, cotangent):
    inputs = tiles[0]
    length, width = inputs.shape
    assert length == SEG and shards % 2 == 0
    spots = shards // 2
    columns = width // shards
    fused = columns % PAD == 0 and columns % (8 * slides) == 0 and spots > 1 and slides > 1
    pairs = ATTENTION_HEADS // 2
    ends = [0] + [count * SPAN // LANES for count in (pairs // 2, pairs - 1, pairs)]
    groups = list(zip(ends[:-1], ends[1:])) if fused else []
    dma = pltpu.SemaphoreType.DMA
    held = pltpu.VMEM((width, length), BF16)
    square = pltpu.VMEM((width, width), BF16)
    tall = pltpu.VMEM((length, width), BF16)
    block = 2 * (length // RATE)
    scratch = [tall] + [square] * 4 + [tall] * 2 + [dma((7,))] + [held] * 5 + [
        pltpu.VMEM((width, block), BF16),
        pltpu.VMEM((2, spots, width, block), BF16),
        pltpu.VMEM((pairs, SPAN + PAD, block), BF16),
        pltpu.VMEM((pairs, length, block), BF16),
        pltpu.VMEM((2, length, SPAN + PAD), BF16),
        pltpu.VMEM((2, SPAN + PAD, length), BF16),
        pltpu.VMEM((2, 8, length), F32),
        pltpu.VMEM((length, length), F32),
        pltpu.VMEM((length, length), F32),
        pltpu.VMEM((length, length), BF16),
        pltpu.VMEM((length, length), BF16),
        dma((2, spots - 1)),
        dma((2, spots - 1)),
        dma((2, spots)),
        dma((2, spots)),
    ]
    grad_type = jax.ShapeDtypeStruct((width, width), BF16)
    if fused:
        grad_type = jax.ShapeDtypeStruct((columns, width), F32)
    for first, last in groups:
        rows = columns * (last - first)
        part = rows // slides
        scratch += [
            pltpu.VMEM((2, spots, rows, LANES), BF16),
            pltpu.VMEM((spots, rows, LANES), BF16),
            dma((1,)),
            dma((1,)),
        ]
        if first == 0:
            scratch += [
                pltpu.VMEM((slides, spots, part, LANES), BF16),
                pltpu.VMEM((slides - 1, spots, part, LANES), BF16),
                pltpu.VMEM((spots, part, LANES), BF16),
                pltpu.VMEM((spots - 1, part, LANES), BF16),
                pltpu.VMEM((slides, part, LANES), BF16),
            ]
            counts = (slides - 1, spots - 1, slides - 1)
        else:
            scratch += [
                pltpu.VMEM((spots, rows, LANES), BF16),
                pltpu.VMEM((spots - 1, rows, LANES), BF16),
                pltpu.VMEM((slides, rows, LANES), BF16),
            ]
            counts = (spots - 1, slides - 1)
        for count in counts:
            scratch += [dma((count,)), dma((count,))]
    hbm = pl.BlockSpec(memory_space=pl.ANY)
    branch_type = jax.ShapeDtypeStruct((length, width), BF16)
    branch, grad = pl.pallas_call(
        functools.partial(attention_kernel, shards, slides, groups),
        out_shape=(branch_type, grad_type),
        in_specs=[SMEM] * 2 + [hbm] * 6,
        out_specs=(hbm, VMEM),
        scratch_shapes=scratch,
        compiler_params=pltpu.CompilerParams(
            vmem_limit_bytes=60 << 20, collective_id=0, has_side_effects=True
        ),
    )(tile_count, offsets, inputs, w_query, w_key, w_value, w_out, cotangent[0])
    if fused:
        branch, grad = pl.pallas_call(
            move_kernel,
            out_shape=(branch_type, grad_type),
            in_specs=[hbm] * 2,
            out_specs=(hbm, hbm),
            scratch_shapes=[tall, pltpu.VMEM((columns, width), F32), dma((9,)), dma((9,))],
        )(branch, grad)
        grad = grad.T
    else:
        share = lax.psum_scatter(grad, "seq", scatter_dimension=0, tiled=True)
        grad = lax.psum(share, "dp").astype(F32).T
    return (branch[None], grad)


def solution(mesh):
    in_specs = (P("dp", "seq", None), P("dp"), P(), P(), P(), P(), P(), P("dp", "seq", None))
    out_specs = (P("dp", "seq", None), P(None, "seq"))
    run = functools.partial(body, mesh.shape["seq"], mesh.shape["dp"])
    return jax.shard_map(run, mesh=mesh, in_specs=in_specs, out_specs=out_specs, check_vma=False)
```

```python
import functools

import jax
import jax.numpy as jnp
from jax import lax
from jax.experimental import pallas as pl
from jax.experimental.pallas import tpu as pltpu
from jax.sharding import PartitionSpec as P

ATTENTION_HEADS = 16
HEAD_SIZE = 48
SEG = 1024
RATE = 16
NEGATIVE_FLOOR = -1e30
LOG2_SCALE = 1.4426950408889634 / HEAD_SIZE**0.5
PAD = 16
SPAN = 2 * HEAD_SIZE
PARTS = 8
LANES = 128
MESH = pl.DeviceIdType.MESH
BF16 = jnp.bfloat16
F32 = jnp.float32
VMEM = pl.BlockSpec(memory_space=pltpu.VMEM)
SMEM = pl.BlockSpec(memory_space=pltpu.SMEM)


def dot(a, b, ca=1, cb=0):
    return lax.dot_general(a, b, (((ca,), (cb,)), ((), ())), preferred_element_type=F32)


def head_rows(head):
    return pl.ds(pl.multiple_of(head * HEAD_SIZE, PAD), HEAD_SIZE)


def scaled_query(query):
    scaled = query.astype(F32) * LOG2_SCALE
    high = scaled.astype(BF16)
    low = (scaled - high.astype(F32)).astype(BF16)
    return jnp.concatenate([high, low, jnp.ones((PAD, query.shape[1]), BF16)], 0)


def masked_key(key, dead):
    row = lax.broadcasted_iota(jnp.int32, (PAD, key.shape[1]), 0)
    mask = jnp.where(dead & (row == 0), NEGATIVE_FLOOR, 0.0).astype(BF16)
    return jnp.concatenate([key, key, mask], 0)


def counted_value(value):
    return jnp.concatenate([value, jnp.ones((PAD, value.shape[1]), BF16)], 0)


def lanes(width):
    return lax.broadcasted_iota(jnp.int32, (PAD, width), 1)


def pair_rows(pair):
    return pl.ds(pl.multiple_of(pair * SPAN, PAD), SPAN)


def grid(shape, axis):
    return lax.broadcasted_iota(jnp.int32, shape, axis)


def pair_offset(lane, picked, offsets, pair):
    first = lane < picked
    return jnp.where(first, lane, lane - picked) * RATE + jnp.where(first, offsets[2 * pair], offsets[2 * pair + 1])


def pick_pair(pair, core, offsets, q, k, v, chosen, queries, onehots):
    length = q.shape[1]
    block = chosen.shape[1]
    picked = block // 2
    rows = pair_rows(pair)
    target = pair_offset(grid((1, block), 1), picked, offsets, pair)
    onehot = jnp.where(grid((length, block), 0) == target, 1.0, 0.0).astype(BF16)
    onehots[pair] = onehot
    part = dot(jnp.concatenate([q[rows, :], k[rows, :], v[rows, :]], 0), onehot)
    left = grid((SPAN, block), 1) < picked
    top = grid((SPAN, block), 0) < HEAD_SIZE
    queries[pair, :SPAN, :] = jnp.where(left == top, part[:SPAN], 0.0).astype(BF16)
    side = jnp.where(grid((PAD, block), 1) < picked, 0, 1)
    queries[pair, SPAN:, :] = jnp.where(grid((PAD, block), 0) == side, 1.0, 0.0).astype(BF16)
    keys, values = part[SPAN : 2 * SPAN], part[2 * SPAN :]
    front = jnp.where(core == 0, keys, values)
    back = jnp.where(core == 0, values, keys)
    front = jnp.where(top, front, pltpu.roll(front, picked, 1))
    back = jnp.where(top, pltpu.roll(back, picked, 1), back)
    chosen[rows, :] = jnp.where(left, front, back).astype(BF16)


def split_level(level):
    high = level.astype(BF16).astype(F32)
    middle = (level - high).astype(BF16).astype(F32)
    return high, middle, level - high - middle


def dilated_pair(pair, me, live, offsets, near, levels, attn, gathered, queries, onehots):
    length = near.shape[1]
    spots, block = gathered.shape[1], gathered.shape[3]
    picked = block // 2
    far = spots * block
    rows = pair_rows(pair)
    left = grid((SPAN, block), 1) < picked
    keys, values = [], []
    for n in range(spots):
        even, odd = gathered[0, n, rows, :], gathered[1, n, rows, :]
        keys.append(jnp.where(left, even, odd))
        values.append(jnp.where(left, odd, even))
    row = grid((PAD, far), 0)
    spot = RATE * grid((PAD, far), 1) + jnp.where(row == 0, offsets[2 * pair], offsets[2 * pair + 1])
    mask = jnp.where((spot >= live) & (row < 2), NEGATIVE_FLOOR, 0.0).astype(BF16)
    key = jnp.concatenate([jnp.concatenate(keys, 1), mask], 0)
    value = counted_value(jnp.concatenate(values, 1))
    scores = dot(key, queries[pair], 0, 0)
    peak = jnp.max(scores, axis=0, keepdims=True)
    weights = jnp.exp2((scores - peak) * LOG2_SCALE).astype(BF16)
    parts = []
    for n in range(spots):
        start = n * block
        parts += [weights[start + picked : start + block], weights[start : start + picked]]
    total = dot(value, jnp.concatenate(parts, 0))
    count = total[SPAN : SPAN + 1]
    far_level = peak * LOG2_SCALE + jnp.log2(count)
    row = grid((PAD, length), 0)
    stats = jnp.zeros((PAD, length), F32)
    for index, item in enumerate(split_level(levels[2 * pair][:1]) + split_level(levels[2 * pair + 1][:1])):
        stats = jnp.where(row == index, item, stats)
    here = near[rows, :]
    mine = dot(jnp.concatenate([here, stats.astype(BF16)], 0), onehots[pair])
    first = mine[SPAN : SPAN + 1] + mine[SPAN + 1 : SPAN + 2] + mine[SPAN + 2 : SPAN + 3]
    second = mine[SPAN + 3 : SPAN + 4] + mine[SPAN + 4 : SPAN + 5] + mine[SPAN + 5 : SPAN + 6]
    level = jnp.where(grid((1, block), 1) < picked, first, second)
    token = pair_offset(grid((1, block), 1), picked, offsets, pair) + me * length
    alive = jnp.where(token < live, 1.0, 0.0)
    near_share = alive / (1.0 + jnp.exp2(far_level - level))
    far_share = alive / (1.0 + jnp.exp2(level - far_level)) / count
    top = grid((SPAN, block), 0) < HEAD_SIZE
    part = jnp.where(left == top, mine[:SPAN] * near_share + total[:SPAN] * far_share, 0.0).astype(BF16)
    spread = dot(part, onehots[pair], 1, 1)
    offset = jnp.where(grid((SPAN, length), 0) < HEAD_SIZE, offsets[2 * pair], offsets[2 * pair + 1])
    is_picked = grid((SPAN, length), 1) % RATE == offset
    attn[rows, :] = jnp.where(is_picked, spread, here.astype(F32)).astype(BF16)


def prepare(head, slot, dead, q, k, keys, scaled):
    rows = head_rows(head)
    scaled[slot] = scaled_query(q[rows, :])
    keys[slot] = masked_key(k[rows, :], dead).T


def local_stage(score, weigh, total_of, dead, levels, v, near, keys, scaled, peaks, scores, weights):
    length = near.shape[1]
    step = length // PARTS
    run, total = None, None
    if weigh is not None:
        peak = peaks[weigh]
    if total_of is not None:
        head, slot = total_of
        rows = head_rows(head)
        value = counted_value(v[rows, :])
        old = peaks[slot]
    for part in range(PARTS):
        cut = slice(part * step, (part + 1) * step)
        if weigh is not None:
            shifted = scores[weigh][cut, :].reshape(step // 8, 8, length) - peak[None]
            weights[weigh][cut, :] = jnp.exp2(shifted.reshape(step, length)).astype(BF16)
        if total_of is not None:
            piece = dot(value[:, cut], weights[slot][cut, :])
            total = piece if total is None else total + piece
        if score is not None:
            here = dot(keys[score, cut, :], scaled[score])
            scores[score][cut, :] = here
            top = jnp.max(here.reshape(step // 8, 8, length), axis=0)
            run = top if run is None else jnp.maximum(run, top)
    if total_of is not None:
        count = total[HEAD_SIZE : HEAD_SIZE + 1]
        levels[head] = old + jnp.log2(count)
        factor = jnp.where(dead[:1], 0.0, 1.0) / count
        near[rows, :] = (total[:HEAD_SIZE] * factor).astype(BF16)
    if score is not None:
        peaks[score] = jnp.broadcast_to(jnp.max(run, axis=0, keepdims=True), (8, length))


def attention_kernel(
    shards, slides, groups, live, offsets, x_hbm, wq_hbm, wk_hbm, wv_hbm, wo_hbm, cot_hbm, branch_hbm, grad,
    x, wq, wk, wv, w_out, cot, branch, loads, q, k, v, near, attn, chosen, gathered, queries, onehots,
    keys, scaled, peaks, levels, s0, s1, w0, w1, line_out, line_here, pair_out, pair_here, *scratch
):
    width, length = q.shape
    pairs = ATTENTION_HEADS // 2
    half = pairs // 2
    cut = half * SPAN
    me = lax.axis_index("seq")
    slide = lax.axis_index("dp")
    spots = shards // 2
    spot, core = me // 2, me % 2
    ahead = [lax.rem(spot + n, spots) for n in range(spots)]
    behind = [lax.rem(spot + spots - n, spots) for n in range(spots)]
    others = [lax.rem(slide + n, slides) for n in range(slides)]
    partner = {"seq": me + 1 - 2 * core}
    line = [{"seq": 2 * ahead[n] + core} for n in range(spots)]
    peers = [partner] + line[1:]
    if groups:
        peers = peers + [{"dp": others[n]} for n in range(1, slides)]
    barrier = pltpu.get_barrier_semaphore()
    for peer in peers:
        pl.semaphore_signal(barrier, inc=1, device_id=peer, device_id_type=MESH)

    def load(index):
        source, target = ((x_hbm, x), (wk_hbm, wk), (wv_hbm, wv), (wq_hbm, wq), (cot_hbm, cot), (wo_hbm, w_out))[index]
        return pltpu.make_async_copy(source, target, loads.at[index])

    for index in range(4):
        load(index).start()

    def copy(src, dst, send, recv, peer):
        item = pltpu.make_async_remote_copy(
            src_ref=src, dst_ref=dst, send_sem=send, recv_sem=recv, device_id=peer, device_id_type=MESH
        )
        item.start()
        return item

    load(0).wait()
    for index, (weight, out) in enumerate(((wk, k), (wv, v), (wq, q))):
        load(index + 1).wait()
        out[...] = dot(weight[...].T, x[...], 1, 1).astype(BF16)
    for index in (4, 5):
        load(index).start()

    def pick(pair, carry):
        pick_pair(pair, core, offsets, q, k, v, chosen, queries, onehots)
        return carry

    def slab(g):
        return pl.ds(g * cut, cut)

    def sent(g, n):
        return pltpu.make_async_remote_copy(
            src_ref=chosen.at[slab(g)],
            dst_ref=gathered.at[core, spot, slab(g)],
            send_sem=line_out.at[g, n - 1],
            recv_sem=line_here.at[g, n - 1],
            device_id=line[n],
            device_id_type=MESH,
        )

    def shared(g, n, side):
        slot = gathered.at[side, behind[n], slab(g)]
        return pltpu.make_async_remote_copy(
            src_ref=slot if n else chosen.at[slab(g)],
            dst_ref=slot,
            send_sem=pair_out.at[g, n],
            recv_sem=pair_here.at[g, n],
            device_id=partner,
            device_id_type=MESH,
        )

    def send_own(g):
        for n in range(1, spots):
            sent(g, n).start()
        shared(g, 0, core).start()

    def share(g):
        for n in range(1, spots):
            slot = gathered.at[core, behind[n], slab(g)]
            pltpu.make_async_remote_copy(
                src_ref=slot,
                dst_ref=slot,
                send_sem=line_out.at[g, n - 1],
                recv_sem=line_here.at[g, n - 1],
                device_id=line[n],
                device_id_type=MESH,
            ).wait_recv()
            shared(g, n, core).start()

    def arrived(g):
        for n in range(spots):
            shared(g, n, 1 - core).wait_recv()

    def end_gather():
        for g in range(2):
            for n in range(spots):
                shared(g, n, core).wait_send()
                if n:
                    sent(g, n).wait_send()

    lax.fori_loop(0, half, pick, 0, unroll=2)
    pl.semaphore_wait(barrier, len(peers))
    send_own(0)
    lax.fori_loop(half, pairs, pick, 0, unroll=2)
    gathered[core, spot] = chosen[...]

    dead = lanes(length) + me * length >= live[0]
    scores, weights = (s0, s1), (w0, w1)

    def advance(score, weigh, total_of):
        local_stage(score, weigh, total_of, dead, levels, v, near, keys, scaled, peaks, scores, weights)

    def block(head, slot):
        prepare(jnp.minimum(head + 2, ATTENTION_HEADS - 2 + slot), slot, dead, q, k, keys, scaled)
        advance(1 - slot, slot, (jnp.maximum(head - 1, 0), 1 - slot))

    def both(index, carry):
        @pl.when(index > -1)
        def _():
            block(2 * index, 0)

        @pl.when(index > -2)
        def _():
            block(2 * index + 1, 1)

        return carry

    def local(start, stop):
        if start % 2 and start < stop:
            block(start, 1)
            start += 1
        lax.fori_loop(start // 2, stop // 2, both, 0)
        if stop % 2 and start < stop:
            block(stop - 1, 0)

    def dilated(pair):
        dilated_pair(pair, me, live[0], offsets, near, levels, attn, gathered, queries, onehots)

    def rest(pair, carry):
        dilated(pair)
        return carry

    def dilated_half(start):
        lax.fori_loop(start, start + half, rest, 0, unroll=half)

    def gradient(rows):
        return dot(attn[rows, :], cot[...]).astype(BF16).T

    stages = []
    used = 0
    for first, last in groups:
        count = 11 if stages else 15
        stages.append(scratch[used : used + count])
        used += count
    columns = width // shards

    def open_pair(g):
        first, last = groups[g]
        stage, pair_in, send, recv = stages[g][:4]
        whole = gradient(slice(first * LANES, last * LANES))
        for shard in range(shards):
            for tile in range(last - first):
                stage[shard % 2, shard // 2, tile * columns : (tile + 1) * columns, :] = whole[
                    shard * columns : (shard + 1) * columns, tile * LANES : (tile + 1) * LANES
                ]
        moves[g, 0] = [copy(stage.at[1 - core], pair_in, send.at[0], recv.at[0], partner)]

    def open_across(g):
        stage, pair_in = stages[g][:2]
        chip, slide_in, send, recv = stages[g][4:6] + stages[g][9:11]
        part = chip.shape[2]
        moves[g, 0][0].wait_recv()
        for n in range(spots):
            mine = stage[core, n].astype(F32) + pair_in[n].astype(F32)
            for p in range(slides):
                chip[p, n] = mine[p * part : (p + 1) * part].astype(BF16)
        moves[g, 1] = [
            copy(chip.at[others[j]], slide_in.at[j - 1], send.at[j - 1], recv.at[j - 1], {"dp": others[j]})
            for j in range(1, slides)
        ]

    def open_along(g):
        chip, slide_in, chip_sum, line_in, send, recv = stages[g][4:8] + stages[g][11:13]
        for item in moves[g, 1]:
            item.wait_recv()
        for n in range(spots):
            total = chip[slide, n].astype(F32)
            for j in range(1, slides):
                total = total + slide_in[j - 1, n].astype(F32)
            chip_sum[n] = total.astype(BF16)
        moves[g, 2] = [
            copy(chip_sum.at[ahead[n]], line_in.at[n - 1], send.at[n - 1], recv.at[n - 1], line[n])
            for n in range(1, spots)
        ]

    def open_last(g):
        chip_sum, line_in, final, send, recv = stages[g][6:9] + stages[g][13:15]
        total = chip_sum[spot].astype(F32)
        for n in range(1, spots):
            moves[g, 2][n - 1].wait_recv()
            total = total + line_in[n - 1].astype(F32)
        final[slide] = total.astype(BF16)
        moves[g, 3] = [
            copy(final.at[slide], final.at[slide], send.at[j - 1], recv.at[j - 1], {"dp": others[j]})
            for j in range(1, slides)
        ]

    def close(g):
        first, last = groups[g]
        final = stages[g][8]
        for item in moves[g, 3]:
            item.wait_recv()
        full = jnp.concatenate([final[p].astype(F32) for p in range(slides)], 0)
        for tile in range(last - first):
            at = (first + tile) * LANES
            grad[:, at : at + LANES] = full[tile * columns : (tile + 1) * columns]

    def short_along(g):
        stage, pair_in = stages[g][:2]
        chip_sum, line_in = stages[g][4:6]
        send, recv = stages[g][7:9]
        moves[g, 0][0].wait_recv()
        for n in range(spots):
            chip_sum[n] = (stage[core, n].astype(F32) + pair_in[n].astype(F32)).astype(BF16)
        moves[g, 2] = [
            copy(chip_sum.at[ahead[n]], line_in.at[n - 1], send.at[n - 1], recv.at[n - 1], line[n])
            for n in range(1, spots)
        ]

    def short_last(g):
        chip_sum, line_in, final = stages[g][4:7]
        send, recv = stages[g][9:11]
        total = chip_sum[spot].astype(F32)
        for n in range(1, spots):
            moves[g, 2][n - 1].wait_recv()
            total = total + line_in[n - 1].astype(F32)
        final[slide] = total.astype(BF16)
        moves[g, 3] = [
            copy(final.at[slide], final.at[slide], send.at[j - 1], recv.at[j - 1], {"dp": others[j]})
            for j in range(1, slides)
        ]

    def short_close(g):
        first, last = groups[g]
        final = stages[g][6]
        for item in moves[g, 3]:
            item.wait_recv()
        full = final[0].astype(F32)
        for p in range(1, slides):
            full = full + final[p].astype(F32)
        for tile in range(last - first):
            at = (first + tile) * LANES
            grad[:, at : at + LANES] = full[tile * columns : (tile + 1) * columns]

    moves = {}
    store = pltpu.make_async_copy(branch, branch_hbm, loads.at[6])

    def project(part, parts):
        rows = slice(part * length // parts, (part + 1) * length // parts)
        branch[rows, :] = dot(attn[:, rows].T, w_out[...]).astype(BF16)

    w1[...] = jnp.ones(w1.shape, BF16)
    peaks[1] = jnp.zeros(peaks.shape[1:], F32)
    prepare(0, 0, dead, q, k, keys, scaled)
    prepare(1, 1, dead, q, k, keys, scaled)
    advance(0, None, None)
    todo = {n: [] for n in range(ATTENTION_HEADS + 1)}
    ready = ATTENTION_HEADS // 2 + 3
    late = ATTENTION_HEADS - 1
    todo[ATTENTION_HEADS // 4].append(functools.partial(send_own, 1))
    todo[ready - 1].append(functools.partial(share, 0))
    todo[ready] += [functools.partial(arrived, 0), functools.partial(dilated_half, 0)]
    todo[late - 1].append(functools.partial(share, 1))
    todo[late].append(functools.partial(arrived, 1))
    if groups:
        todo[ready] += [load(4).wait, functools.partial(open_pair, 0)]
        todo[ready + 1].append(functools.partial(open_across, 0))
    done = 0
    for at in range(ATTENTION_HEADS + 1):
        if todo[at]:
            local(done, at)
            done = at
            for action in todo[at]:
                action()

    if not groups:
        local(done, ATTENTION_HEADS)
        advance(None, None, (ATTENTION_HEADS - 1, 1))
        dilated_half(half)
        load(4).wait()
        load(5).wait()
        grad[...] = gradient(slice(0, width))
        project(0, 1)
        store.start()
        end_gather()
        store.wait()
        return

    lax.fori_loop(half, pairs - 1, rest, 0, unroll=3)
    open_pair(1)
    open_along(0)
    local(done, ATTENTION_HEADS)
    short_along(1)
    advance(None, None, (ATTENTION_HEADS - 1, 1))
    dilated(pairs - 1)
    open_pair(2)
    load(5).wait()
    project(0, 2)
    short_along(2)
    open_last(0)
    project(1, 2)
    store.start()
    short_last(1)
    short_last(2)
    close(0)
    short_close(1)
    end_gather()
    short_close(2)
    for items in moves.values():
        for item in items:
            item.wait_send()
    store.wait()


def move_kernel(branch, grad, branch_out, grad_out, held, small, come, leave):
    length = branch.shape[0]
    parts = come.shape[0] - 1
    pieces = [(grad, small, grad_out)]
    for n in range(parts):
        rows = pl.ds(n * (length // parts), length // parts)
        pieces.append((branch.at[rows], held.at[rows], branch_out.at[rows]))
    loads = [pltpu.make_async_copy(a, b, come.at[n]) for n, (a, b, c) in enumerate(pieces)]
    stores = [pltpu.make_async_copy(b, c, leave.at[n]) for n, (a, b, c) in enumerate(pieces)]
    for item in loads:
        item.start()
    for item, out in zip(loads, stores):
        item.wait()
        out.start()
    for item in stores:
        item.wait()


def body(shards, slides, tiles, tile_count, offsets, w_query, w_key, w_value, w_out, cotangent):
    inputs = tiles[0]
    length, width = inputs.shape
    assert length == SEG and shards % 2 == 0
    spots = shards // 2
    columns = width // shards
    fused = columns % PAD == 0 and columns % (8 * slides) == 0 and spots > 1 and slides > 1
    pairs = ATTENTION_HEADS // 2
    ends = [0] + [count * SPAN // LANES for count in (pairs // 2, pairs - 1, pairs)]
    groups = list(zip(ends[:-1], ends[1:])) if fused else []
    dma = pltpu.SemaphoreType.DMA
    held = pltpu.VMEM((width, length), BF16)
    square = pltpu.VMEM((width, width), BF16)
    tall = pltpu.VMEM((length, width), BF16)
    block = 2 * (length // RATE)
    scratch = [tall] + [square] * 4 + [tall] * 2 + [dma((7,))] + [held] * 5 + [
        pltpu.VMEM((width, block), BF16),
        pltpu.VMEM((2, spots, width, block), BF16),
        pltpu.VMEM((pairs, SPAN + PAD, block), BF16),
        pltpu.VMEM((pairs, length, block), BF16),
        pltpu.VMEM((2, length, SPAN + PAD), BF16),
        pltpu.VMEM((2, SPAN + PAD, length), BF16),
        pltpu.VMEM((2, 8, length), F32),
        pltpu.VMEM((ATTENTION_HEADS, 8, length), F32),
        pltpu.VMEM((length, length), F32),
        pltpu.VMEM((length, length), F32),
        pltpu.VMEM((length, length), BF16),
        pltpu.VMEM((length, length), BF16),
        dma((2, spots - 1)),
        dma((2, spots - 1)),
        dma((2, spots)),
        dma((2, spots)),
    ]
    grad_type = jax.ShapeDtypeStruct((width, width), BF16)
    if fused:
        grad_type = jax.ShapeDtypeStruct((columns, width), F32)
    for first, last in groups:
        rows = columns * (last - first)
        part = rows // slides
        scratch += [
            pltpu.VMEM((2, spots, rows, LANES), BF16),
            pltpu.VMEM((spots, rows, LANES), BF16),
            dma((1,)),
            dma((1,)),
        ]
        if first == 0:
            scratch += [
                pltpu.VMEM((slides, spots, part, LANES), BF16),
                pltpu.VMEM((slides - 1, spots, part, LANES), BF16),
                pltpu.VMEM((spots, part, LANES), BF16),
                pltpu.VMEM((spots - 1, part, LANES), BF16),
                pltpu.VMEM((slides, part, LANES), BF16),
            ]
            counts = (slides - 1, spots - 1, slides - 1)
        else:
            scratch += [
                pltpu.VMEM((spots, rows, LANES), BF16),
                pltpu.VMEM((spots - 1, rows, LANES), BF16),
                pltpu.VMEM((slides, rows, LANES), BF16),
            ]
            counts = (spots - 1, slides - 1)
        for count in counts:
            scratch += [dma((count,)), dma((count,))]
    hbm = pl.BlockSpec(memory_space=pl.ANY)
    branch_type = jax.ShapeDtypeStruct((length, width), BF16)
    branch, grad = pl.pallas_call(
        functools.partial(attention_kernel, shards, slides, groups),
        out_shape=(branch_type, grad_type),
        in_specs=[SMEM] * 2 + [hbm] * 6,
        out_specs=(hbm, VMEM),
        scratch_shapes=scratch,
        compiler_params=pltpu.CompilerParams(
            vmem_limit_bytes=60 << 20, collective_id=0, has_side_effects=True
        ),
    )(tile_count, offsets, inputs, w_query, w_key, w_value, w_out, cotangent[0])
    if fused:
        branch, grad = pl.pallas_call(
            move_kernel,
            out_shape=(branch_type, grad_type),
            in_specs=[hbm] * 2,
            out_specs=(hbm, hbm),
            scratch_shapes=[tall, pltpu.VMEM((columns, width), F32), dma((5,)), dma((5,))],
        )(branch, grad)
        grad = grad.T
    else:
        share = lax.psum_scatter(grad, "seq", scatter_dimension=0, tiled=True)
        grad = lax.psum(share, "dp").astype(F32).T
    return (branch[None], grad)


def solution(mesh):
    in_specs = (P("dp", "seq", None), P("dp"), P(), P(), P(), P(), P(), P("dp", "seq", None))
    out_specs = (P("dp", "seq", None), P(None, "seq"))
    run = functools.partial(body, mesh.shape["seq"], mesh.shape["dp"])
    return jax.shard_map(run, mesh=mesh, in_specs=in_specs, out_specs=out_specs, check_vma=False)
```

```python
import functools

import jax
import jax.numpy as jnp
from jax import lax
from jax.experimental import pallas as pl
from jax.experimental.pallas import tpu as pltpu
from jax.sharding import PartitionSpec as P

ATTENTION_HEADS = 16
HEAD_SIZE = 48
SEG = 1024
RATE = 16
NEGATIVE_FLOOR = -1e30
LOG2_SCALE = 1.4426950408889634 / HEAD_SIZE**0.5
PAD = 16
SPAN = 2 * HEAD_SIZE
PARTS = 8
LANES = 128
MESH = pl.DeviceIdType.MESH
BF16 = jnp.bfloat16
F32 = jnp.float32
VMEM = pl.BlockSpec(memory_space=pltpu.VMEM)
SMEM = pl.BlockSpec(memory_space=pltpu.SMEM)


def dot(a, b, ca=1, cb=0):
    return lax.dot_general(a, b, (((ca,), (cb,)), ((), ())), preferred_element_type=F32)


def head_rows(head):
    return pl.ds(pl.multiple_of(head * HEAD_SIZE, PAD), HEAD_SIZE)


def scaled_query(query):
    scaled = query.astype(F32) * LOG2_SCALE
    high = scaled.astype(BF16)
    low = (scaled - high.astype(F32)).astype(BF16)
    return jnp.concatenate([high, low, jnp.ones((PAD, query.shape[1]), BF16)], 0)


def masked_key(key, dead):
    row = lax.broadcasted_iota(jnp.int32, (PAD, key.shape[1]), 0)
    mask = jnp.where(dead & (row == 0), NEGATIVE_FLOOR, 0.0).astype(BF16)
    return jnp.concatenate([key, key, mask], 0)


def counted_value(value):
    return jnp.concatenate([value, jnp.ones((PAD, value.shape[1]), BF16)], 0)


def lanes(width):
    return lax.broadcasted_iota(jnp.int32, (PAD, width), 1)


def pair_rows(pair):
    return pl.ds(pl.multiple_of(pair * SPAN, PAD), SPAN)


def grid(shape, axis):
    return lax.broadcasted_iota(jnp.int32, shape, axis)


def pair_offset(lane, picked, offsets, pair):
    first = lane < picked
    return jnp.where(first, lane, lane - picked) * RATE + jnp.where(first, offsets[2 * pair], offsets[2 * pair + 1])


def pick_pair(pair, core, offsets, q, k, v, chosen, queries, onehots):
    length = q.shape[1]
    block = chosen.shape[1]
    picked = block // 2
    rows = pair_rows(pair)
    target = pair_offset(grid((1, block), 1), picked, offsets, pair)
    onehot = jnp.where(grid((length, block), 0) == target, 1.0, 0.0).astype(BF16)
    onehots[pair] = onehot
    part = dot(jnp.concatenate([q[rows, :], k[rows, :], v[rows, :]], 0), onehot)
    left = grid((SPAN, block), 1) < picked
    top = grid((SPAN, block), 0) < HEAD_SIZE
    queries[pair, :SPAN, :] = jnp.where(left == top, part[:SPAN], 0.0).astype(BF16)
    side = jnp.where(grid((PAD, block), 1) < picked, 0, 1)
    queries[pair, SPAN:, :] = jnp.where(grid((PAD, block), 0) == side, 1.0, 0.0).astype(BF16)
    keys, values = part[SPAN : 2 * SPAN], part[2 * SPAN :]
    front = jnp.where(core == 0, keys, values)
    back = jnp.where(core == 0, values, keys)
    front = jnp.where(top, front, pltpu.roll(front, picked, 1))
    back = jnp.where(top, pltpu.roll(back, picked, 1), back)
    chosen[rows, :] = jnp.where(left, front, back).astype(BF16)


def split_level(level):
    high = level.astype(BF16).astype(F32)
    middle = (level - high).astype(BF16).astype(F32)
    return high, middle, level - high - middle


def dilated_pair(pair, me, live, offsets, near, levels, attn, gathered, queries, onehots):
    length = near.shape[1]
    spots, block = gathered.shape[1], gathered.shape[3]
    picked = block // 2
    far = spots * block
    rows = pair_rows(pair)
    left = grid((SPAN, block), 1) < picked
    keys, values = [], []
    for n in range(spots):
        even, odd = gathered[0, n, rows, :], gathered[1, n, rows, :]
        keys.append(jnp.where(left, even, odd))
        values.append(jnp.where(left, odd, even))
    row = grid((PAD, far), 0)
    spot = RATE * grid((PAD, far), 1) + jnp.where(row == 0, offsets[2 * pair], offsets[2 * pair + 1])
    mask = jnp.where((spot >= live) & (row < 2), NEGATIVE_FLOOR, 0.0).astype(BF16)
    key = jnp.concatenate([jnp.concatenate(keys, 1), mask], 0)
    value = counted_value(jnp.concatenate(values, 1))
    scores = dot(key, queries[pair], 0, 0)
    peak = jnp.max(scores, axis=0, keepdims=True)
    weights = jnp.exp2((scores - peak) * LOG2_SCALE).astype(BF16)
    parts = []
    for n in range(spots):
        start = n * block
        parts += [weights[start + picked : start + block], weights[start : start + picked]]
    total = dot(value, jnp.concatenate(parts, 0))
    count = total[SPAN : SPAN + 1]
    far_level = peak * LOG2_SCALE + jnp.log2(count)
    row = grid((PAD, length), 0)
    stats = jnp.zeros((PAD, length), F32)
    for index, item in enumerate(split_level(levels[2 * pair][:1]) + split_level(levels[2 * pair + 1][:1])):
        stats = jnp.where(row == index, item, stats)
    here = near[rows, :]
    mine = dot(jnp.concatenate([here, stats.astype(BF16)], 0), onehots[pair])
    first = mine[SPAN : SPAN + 1] + mine[SPAN + 1 : SPAN + 2] + mine[SPAN + 2 : SPAN + 3]
    second = mine[SPAN + 3 : SPAN + 4] + mine[SPAN + 4 : SPAN + 5] + mine[SPAN + 5 : SPAN + 6]
    level = jnp.where(grid((1, block), 1) < picked, first, second)
    token = pair_offset(grid((1, block), 1), picked, offsets, pair) + me * length
    alive = jnp.where(token < live, 1.0, 0.0)
    near_share = alive / (1.0 + jnp.exp2(far_level - level))
    far_share = alive / (1.0 + jnp.exp2(level - far_level)) / count
    top = grid((SPAN, block), 0) < HEAD_SIZE
    part = jnp.where(left == top, mine[:SPAN] * near_share + total[:SPAN] * far_share, 0.0).astype(BF16)
    spread = dot(part, onehots[pair], 1, 1)
    offset = jnp.where(grid((SPAN, length), 0) < HEAD_SIZE, offsets[2 * pair], offsets[2 * pair + 1])
    is_picked = grid((SPAN, length), 1) % RATE == offset
    attn[rows, :] = jnp.where(is_picked, spread, here.astype(F32)).astype(BF16)


def prepare(head, slot, dead, q, k, keys, scaled):
    rows = head_rows(head)
    scaled[slot] = scaled_query(q[rows, :])
    keys[slot] = masked_key(k[rows, :], dead).T


def local_stage(score, weigh, total_of, dead, levels, v, near, keys, scaled, peaks, scores, weights):
    length = near.shape[1]
    step = length // PARTS
    run, total = None, None
    if weigh is not None:
        peak = peaks[weigh]
    if total_of is not None:
        head, slot = total_of
        rows = head_rows(head)
        value = counted_value(v[rows, :])
        old = peaks[slot]
    for part in range(PARTS):
        cut = slice(part * step, (part + 1) * step)
        if weigh is not None:
            shifted = scores[weigh][cut, :].reshape(step // 8, 8, length) - peak[None]
            weights[weigh][cut, :] = jnp.exp2(shifted.reshape(step, length)).astype(BF16)
        if total_of is not None:
            piece = dot(value[:, cut], weights[slot][cut, :])
            total = piece if total is None else total + piece
        if score is not None:
            here = dot(keys[score, cut, :], scaled[score])
            scores[score][cut, :] = here
            top = jnp.max(here.reshape(step // 8, 8, length), axis=0)
            run = top if run is None else jnp.maximum(run, top)
    if total_of is not None:
        count = total[HEAD_SIZE : HEAD_SIZE + 1]
        levels[head] = old + jnp.log2(count)
        factor = jnp.where(dead[:1], 0.0, 1.0) / count
        near[rows, :] = (total[:HEAD_SIZE] * factor).astype(BF16)
    if score is not None:
        peaks[score] = jnp.broadcast_to(jnp.max(run, axis=0, keepdims=True), (8, length))


def attention_kernel(
    shards, slides, groups, live, offsets, x_hbm, wq_hbm, wk_hbm, wv_hbm, wo_hbm, cot_hbm, branch_hbm, grad,
    x, wq, wk, wv, w_out, cot, branch, loads, q, k, v, near, attn, chosen, gathered, queries, onehots,
    keys, scaled, peaks, levels, s0, s1, w0, w1, line_out, line_here, pair_out, pair_here, *scratch
):
    width, length = q.shape
    pairs = ATTENTION_HEADS // 2
    half = pairs // 2
    cut = half * SPAN
    me = lax.axis_index("seq")
    slide = lax.axis_index("dp")
    spots = shards // 2
    spot, core = me // 2, me % 2
    ahead = [lax.rem(spot + n, spots) for n in range(spots)]
    behind = [lax.rem(spot + spots - n, spots) for n in range(spots)]
    others = [lax.rem(slide + n, slides) for n in range(slides)]
    partner = {"seq": me + 1 - 2 * core}
    line = [{"seq": 2 * ahead[n] + core} for n in range(spots)]
    peers = [partner] + line[1:]
    if groups:
        peers = peers + [{"dp": others[n]} for n in range(1, slides)]
    barrier = pltpu.get_barrier_semaphore()
    for peer in peers:
        pl.semaphore_signal(barrier, inc=1, device_id=peer, device_id_type=MESH)

    def load(index):
        source, target = ((x_hbm, x), (wk_hbm, wk), (wv_hbm, wv), (wq_hbm, wq), (cot_hbm, cot), (wo_hbm, w_out))[index]
        return pltpu.make_async_copy(source, target, loads.at[index])

    for index in range(4):
        load(index).start()

    def copy(src, dst, send, recv, peer):
        item = pltpu.make_async_remote_copy(
            src_ref=src, dst_ref=dst, send_sem=send, recv_sem=recv, device_id=peer, device_id_type=MESH
        )
        item.start()
        return item

    load(0).wait()
    for index, (weight, out) in enumerate(((wk, k), (wv, v), (wq, q))):
        load(index + 1).wait()
        out[...] = dot(weight[...].T, x[...], 1, 1).astype(BF16)
    for index in (4, 5):
        load(index).start()

    def pick(pair, carry):
        pick_pair(pair, core, offsets, q, k, v, chosen, queries, onehots)
        return carry

    def slab(g):
        return pl.ds(g * cut, cut)

    def sent(g, n):
        return pltpu.make_async_remote_copy(
            src_ref=chosen.at[slab(g)],
            dst_ref=gathered.at[core, spot, slab(g)],
            send_sem=line_out.at[g, n - 1],
            recv_sem=line_here.at[g, n - 1],
            device_id=line[n],
            device_id_type=MESH,
        )

    def shared(g, n, side):
        slot = gathered.at[side, behind[n], slab(g)]
        return pltpu.make_async_remote_copy(
            src_ref=slot if n else chosen.at[slab(g)],
            dst_ref=slot,
            send_sem=pair_out.at[g, n],
            recv_sem=pair_here.at[g, n],
            device_id=partner,
            device_id_type=MESH,
        )

    def send_own(g):
        for n in range(1, spots):
            sent(g, n).start()
        shared(g, 0, core).start()

    def share(g):
        for n in range(1, spots):
            slot = gathered.at[core, behind[n], slab(g)]
            pltpu.make_async_remote_copy(
                src_ref=slot,
                dst_ref=slot,
                send_sem=line_out.at[g, n - 1],
                recv_sem=line_here.at[g, n - 1],
                device_id=line[n],
                device_id_type=MESH,
            ).wait_recv()
            shared(g, n, core).start()

    def arrived(g):
        for n in range(spots):
            shared(g, n, 1 - core).wait_recv()

    def end_gather():
        for g in range(2):
            for n in range(spots):
                shared(g, n, core).wait_send()
                if n:
                    sent(g, n).wait_send()

    lax.fori_loop(0, half, pick, 0, unroll=2)
    pl.semaphore_wait(barrier, len(peers))
    send_own(0)
    lax.fori_loop(half, pairs, pick, 0, unroll=2)
    gathered[core, spot] = chosen[...]

    dead = lanes(length) + me * length >= live[0]
    scores, weights = (s0, s1), (w0, w1)

    def advance(score, weigh, total_of):
        local_stage(score, weigh, total_of, dead, levels, v, near, keys, scaled, peaks, scores, weights)

    def block(head, slot):
        prepare(jnp.minimum(head + 2, ATTENTION_HEADS - 2 + slot), slot, dead, q, k, keys, scaled)
        advance(1 - slot, slot, (jnp.maximum(head - 1, 0), 1 - slot))

    def both(index, carry):
        @pl.when(index > -1)
        def _():
            block(2 * index, 0)

        @pl.when(index > -2)
        def _():
            block(2 * index + 1, 1)

        return carry

    def local(start, stop):
        if start % 2 and start < stop:
            block(start, 1)
            start += 1
        lax.fori_loop(start // 2, stop // 2, both, 0)
        if stop % 2 and start < stop:
            block(stop - 1, 0)

    def dilated(pair):
        dilated_pair(pair, me, live[0], offsets, near, levels, attn, gathered, queries, onehots)

    def rest(pair, carry):
        dilated(pair)
        return carry

    def dilated_half(start):
        lax.fori_loop(start, start + half, rest, 0, unroll=half)

    def gradient(rows):
        return dot(attn[rows, :], cot[...]).astype(BF16).T

    stages = []
    used = 0
    for first, last in groups:
        count = 11 if stages else 15
        stages.append(scratch[used : used + count])
        used += count
    columns = width // shards

    def open_pair(g):
        first, last = groups[g]
        stage, pair_in, send, recv = stages[g][:4]
        whole = gradient(slice(first * LANES, last * LANES))
        for shard in range(shards):
            for tile in range(last - first):
                stage[shard % 2, shard // 2, tile * columns : (tile + 1) * columns, :] = whole[
                    shard * columns : (shard + 1) * columns, tile * LANES : (tile + 1) * LANES
                ]
        moves[g, 0] = [copy(stage.at[1 - core], pair_in, send.at[0], recv.at[0], partner)]

    def open_across(g):
        stage, pair_in = stages[g][:2]
        chip, slide_in, send, recv = stages[g][4:6] + stages[g][9:11]
        part = chip.shape[2]
        moves[g, 0][0].wait_recv()
        for n in range(spots):
            mine = stage[core, n].astype(F32) + pair_in[n].astype(F32)
            for p in range(slides):
                chip[p, n] = mine[p * part : (p + 1) * part].astype(BF16)
        moves[g, 1] = [
            copy(chip.at[others[j]], slide_in.at[j - 1], send.at[j - 1], recv.at[j - 1], {"dp": others[j]})
            for j in range(1, slides)
        ]

    def open_along(g):
        chip, slide_in, chip_sum, line_in, send, recv = stages[g][4:8] + stages[g][11:13]
        for item in moves[g, 1]:
            item.wait_recv()
        for n in range(spots):
            total = chip[slide, n].astype(F32)
            for j in range(1, slides):
                total = total + slide_in[j - 1, n].astype(F32)
            chip_sum[n] = total.astype(BF16)
        moves[g, 2] = [
            copy(chip_sum.at[ahead[n]], line_in.at[n - 1], send.at[n - 1], recv.at[n - 1], line[n])
            for n in range(1, spots)
        ]

    def open_last(g):
        chip_sum, line_in, final, send, recv = stages[g][6:9] + stages[g][13:15]
        total = chip_sum[spot].astype(F32)
        for n in range(1, spots):
            moves[g, 2][n - 1].wait_recv()
            total = total + line_in[n - 1].astype(F32)
        final[slide] = total.astype(BF16)
        moves[g, 3] = [
            copy(final.at[slide], final.at[slide], send.at[j - 1], recv.at[j - 1], {"dp": others[j]})
            for j in range(1, slides)
        ]

    def close(g):
        first, last = groups[g]
        final = stages[g][8]
        for item in moves[g, 3]:
            item.wait_recv()
        full = jnp.concatenate([final[p].astype(F32) for p in range(slides)], 0)
        for tile in range(last - first):
            at = (first + tile) * LANES
            grad[:, at : at + LANES] = full[tile * columns : (tile + 1) * columns]

    def short_along(g):
        stage, pair_in = stages[g][:2]
        chip_sum, line_in = stages[g][4:6]
        send, recv = stages[g][7:9]
        moves[g, 0][0].wait_recv()
        for n in range(spots):
            chip_sum[n] = (stage[core, n].astype(F32) + pair_in[n].astype(F32)).astype(BF16)
        moves[g, 2] = [
            copy(chip_sum.at[ahead[n]], line_in.at[n - 1], send.at[n - 1], recv.at[n - 1], line[n])
            for n in range(1, spots)
        ]

    def short_last(g):
        chip_sum, line_in, final = stages[g][4:7]
        send, recv = stages[g][9:11]
        total = chip_sum[spot].astype(F32)
        for n in range(1, spots):
            moves[g, 2][n - 1].wait_recv()
            total = total + line_in[n - 1].astype(F32)
        final[slide] = total.astype(BF16)
        moves[g, 3] = [
            copy(final.at[slide], final.at[slide], send.at[j - 1], recv.at[j - 1], {"dp": others[j]})
            for j in range(1, slides)
        ]

    def short_close(g):
        first, last = groups[g]
        final = stages[g][6]
        for item in moves[g, 3]:
            item.wait_recv()
        full = final[0].astype(F32)
        for p in range(1, slides):
            full = full + final[p].astype(F32)
        for tile in range(last - first):
            at = (first + tile) * LANES
            grad[:, at : at + LANES] = full[tile * columns : (tile + 1) * columns]

    moves = {}
    store = pltpu.make_async_copy(branch, branch_hbm, loads.at[6])

    def project(part, parts):
        rows = slice(part * length // parts, (part + 1) * length // parts)
        branch[rows, :] = dot(attn[:, rows].T, w_out[...]).astype(BF16)

    w1[...] = jnp.ones(w1.shape, BF16)
    peaks[1] = jnp.zeros(peaks.shape[1:], F32)
    prepare(0, 0, dead, q, k, keys, scaled)
    prepare(1, 1, dead, q, k, keys, scaled)
    advance(0, None, None)
    todo = {n: [] for n in range(ATTENTION_HEADS + 1)}
    ready = ATTENTION_HEADS // 2 + 4
    late = ATTENTION_HEADS - 1
    todo[ATTENTION_HEADS // 4].append(functools.partial(send_own, 1))
    todo[ready - 1].append(functools.partial(share, 0))
    todo[ready] += [functools.partial(arrived, 0), functools.partial(dilated_half, 0)]
    todo[late - 1].append(functools.partial(share, 1))
    todo[late].append(functools.partial(arrived, 1))
    if groups:
        todo[ready] += [load(4).wait, functools.partial(open_pair, 0)]
        todo[ready + 1].append(functools.partial(open_across, 0))
    done = 0
    for at in range(ATTENTION_HEADS + 1):
        if todo[at]:
            local(done, at)
            done = at
            for action in todo[at]:
                action()

    if not groups:
        local(done, ATTENTION_HEADS)
        advance(None, None, (ATTENTION_HEADS - 1, 1))
        dilated_half(half)
        load(4).wait()
        load(5).wait()
        grad[...] = gradient(slice(0, width))
        project(0, 1)
        store.start()
        end_gather()
        store.wait()
        return

    lax.fori_loop(half, pairs - 1, rest, 0, unroll=3)
    open_pair(1)
    open_along(0)
    local(done, ATTENTION_HEADS)
    short_along(1)
    advance(None, None, (ATTENTION_HEADS - 1, 1))
    dilated(pairs - 1)
    open_pair(2)
    load(5).wait()
    project(0, 2)
    short_along(2)
    open_last(0)
    project(1, 2)
    store.start()
    short_last(1)
    short_last(2)
    close(0)
    short_close(1)
    end_gather()
    short_close(2)
    for items in moves.values():
        for item in items:
            item.wait_send()
    store.wait()


def move_kernel(branch, grad, branch_out, grad_out, held, small, come, leave):
    length = branch.shape[0]
    parts = come.shape[0] - 1
    pieces = [(grad, small, grad_out)]
    for n in range(parts):
        rows = pl.ds(n * (length // parts), length // parts)
        pieces.append((branch.at[rows], held.at[rows], branch_out.at[rows]))
    loads = [pltpu.make_async_copy(a, b, come.at[n]) for n, (a, b, c) in enumerate(pieces)]
    stores = [pltpu.make_async_copy(b, c, leave.at[n]) for n, (a, b, c) in enumerate(pieces)]
    for item in loads:
        item.start()
    for item, out in zip(loads, stores):
        item.wait()
        out.start()
    for item in stores:
        item.wait()


def body(shards, slides, tiles, tile_count, offsets, w_query, w_key, w_value, w_out, cotangent):
    inputs = tiles[0]
    length, width = inputs.shape
    assert length == SEG and shards % 2 == 0
    spots = shards // 2
    columns = width // shards
    fused = columns % PAD == 0 and columns % (8 * slides) == 0 and spots > 1 and slides > 1
    pairs = ATTENTION_HEADS // 2
    ends = [0] + [count * SPAN // LANES for count in (pairs // 2, pairs - 1, pairs)]
    groups = list(zip(ends[:-1], ends[1:])) if fused else []
    dma = pltpu.SemaphoreType.DMA
    held = pltpu.VMEM((width, length), BF16)
    square = pltpu.VMEM((width, width), BF16)
    tall = pltpu.VMEM((length, width), BF16)
    block = 2 * (length // RATE)
    scratch = [tall] + [square] * 4 + [tall] * 2 + [dma((7,))] + [held] * 5 + [
        pltpu.VMEM((width, block), BF16),
        pltpu.VMEM((2, spots, width, block), BF16),
        pltpu.VMEM((pairs, SPAN + PAD, block), BF16),
        pltpu.VMEM((pairs, length, block), BF16),
        pltpu.VMEM((2, length, SPAN + PAD), BF16),
        pltpu.VMEM((2, SPAN + PAD, length), BF16),
        pltpu.VMEM((2, 8, length), F32),
        pltpu.VMEM((ATTENTION_HEADS, 8, length), F32),
        pltpu.VMEM((length, length), F32),
        pltpu.VMEM((length, length), F32),
        pltpu.VMEM((length, length), BF16),
        pltpu.VMEM((length, length), BF16),
        dma((2, spots - 1)),
        dma((2, spots - 1)),
        dma((2, spots)),
        dma((2, spots)),
    ]
    grad_type = jax.ShapeDtypeStruct((width, width), BF16)
    if fused:
        grad_type = jax.ShapeDtypeStruct((columns, width), F32)
    for first, last in groups:
        rows = columns * (last - first)
        part = rows // slides
        scratch += [
            pltpu.VMEM((2, spots, rows, LANES), BF16),
            pltpu.VMEM((spots, rows, LANES), BF16),
            dma((1,)),
            dma((1,)),
        ]
        if first == 0:
            scratch += [
                pltpu.VMEM((slides, spots, part, LANES), BF16),
                pltpu.VMEM((slides - 1, spots, part, LANES), BF16),
                pltpu.VMEM((spots, part, LANES), BF16),
                pltpu.VMEM((spots - 1, part, LANES), BF16),
                pltpu.VMEM((slides, part, LANES), BF16),
            ]
            counts = (slides - 1, spots - 1, slides - 1)
        else:
            scratch += [
                pltpu.VMEM((spots, rows, LANES), BF16),
                pltpu.VMEM((spots - 1, rows, LANES), BF16),
                pltpu.VMEM((slides, rows, LANES), BF16),
            ]
            counts = (spots - 1, slides - 1)
        for count in counts:
            scratch += [dma((count,)), dma((count,))]
    hbm = pl.BlockSpec(memory_space=pl.ANY)
    branch_type = jax.ShapeDtypeStruct((length, width), BF16)
    branch, grad = pl.pallas_call(
        functools.partial(attention_kernel, shards, slides, groups),
        out_shape=(branch_type, grad_type),
        in_specs=[SMEM] * 2 + [hbm] * 6,
        out_specs=(hbm, VMEM),
        scratch_shapes=scratch,
        compiler_params=pltpu.CompilerParams(
            vmem_limit_bytes=60 << 20, collective_id=0, has_side_effects=True
        ),
    )(tile_count, offsets, inputs, w_query, w_key, w_value, w_out, cotangent[0])
    if fused:
        branch, grad = pl.pallas_call(
            move_kernel,
            out_shape=(branch_type, grad_type),
            in_specs=[hbm] * 2,
            out_specs=(hbm, hbm),
            scratch_shapes=[tall, pltpu.VMEM((columns, width), F32), dma((5,)), dma((5,))],
        )(branch, grad)
        grad = grad.T
    else:
        share = lax.psum_scatter(grad, "seq", scatter_dimension=0, tiled=True)
        grad = lax.psum(share, "dp").astype(F32).T
    return (branch[None], grad)


def solution(mesh):
    in_specs = (P("dp", "seq", None), P("dp"), P(), P(), P(), P(), P(), P("dp", "seq", None))
    out_specs = (P("dp", "seq", None), P(None, "seq"))
    run = functools.partial(body, mesh.shape["seq"], mesh.shape["dp"])
    return jax.shard_map(run, mesh=mesh, in_specs=in_specs, out_specs=out_specs, check_vma=False)
```
